32 devices in a mesh: psg: 8 (over y, x, core), qry: 4 (over z).
Axes of the slice: x: 2, y: 2, z: 4, core: 2. Of those that a mesh axis runs over, the one named last changes fastest.
Arguments:
- hidden: bfloat16 [512, 4096], P('qry'), may hold values from -6 to 6
- norm_gain: float32 [4096], replicated, may hold values from 0.5 to 1.5
- proj_weight: bfloat16 [4096, 4096], P('psg', 'qry'), may hold values from -0.09375 to 0.09375
- pq_codes: int32 [16384, 512], P('psg', 'qry'), may hold values from 0 to 255
- codebook: bfloat16 [512, 8, 256], P('qry'), may hold values from -560 to 560
- positives: int32 [512], replicated, may hold values from 0 to 16383
Outputs:
- losses: float32 [512], P('qry')
- hidden_grad: bfloat16 [512, 4096], P('qry')
- weight_grad: float32 [4096, 4096], P('psg', 'qry')
- codebook_grad: float32 [512, 8, 256], P('qry')
The draws below stay inside these ranges and needn't reach their ends.
All inputs are finite; a program needn't handle non-finite values.
Results may differ from the reference program's by a relative error of at most 0.019.
The reference program's roundings to bfloat16 on the way (of `normed`, `queries`, `passages`, `score_grad`, `query_grad` and `passage_grad`) count: a program that leaves them out, or rounds other values in their place, can miss the bound.
Values may be sent and summed in bfloat16 or wider, within the bound.
No kernel may reach another device: no remote copies, remote signals or barrier semaphores. Data moves between devices by JAX's collectives and lax.ppermute only.
A program may use at most 128 MiB of HBM per device.

```python
import math
import jax
import jax.numpy as jnp
from jax import lax

D = 4096
SUB = 8
K = 256
M = 512
Q = 512
PSG_TOTAL = 16384
N_QRY = 4


def draw_codebook(key, part):
    first_key, second_key = jax.random.split(jax.random.fold_in(key, 11), 2)
    root = math.sqrt(D)
    centre_scale = 1280.0 / root
    noise_scale = 48.0 / root
    centre = jnp.clip(jax.random.normal(first_key, (M, SUB, 1), jnp.float32), -3.0, 3.0) * centre_scale
    noise = jnp.clip(jax.random.normal(second_key, (M, SUB, K), jnp.float32), -4.0, 4.0) * noise_scale
    return jnp.clip(centre + noise, -560.0, 560.0).astype(jnp.bfloat16)


def place_ends(entries, own_key, low, largest):
    longest = entries.shape.index(max(entries.shape))
    spots = []
    for shift in (0, 1):
        where = [jax.random.randint(jax.random.fold_in(own_key, axis), (), 0, length) for axis, length in enumerate(entries.shape)]
        where[longest] = (where[longest] + shift) % entries.shape[longest]
        spots.append(tuple(where))
    return entries.at[spots[0]].set(low).at[spots[1]].set(largest)


def steps_of(own_key, shape, cuts, low, high):
    factor_of, own = 1.0, jax.random.fold_in(own_key, 6)
    for position, shards_of in cuts:
        heights = jnp.exp(jax.random.uniform(jax.random.fold_in(own, position), (shards_of,), jnp.float32, low / len(cuts), high / len(cuts)))
        factor_of = factor_of * jnp.repeat(heights, shape[position] // shards_of).reshape([-1 if axis == position else 1 for axis in range(len(shape))])
    return factor_of


def normal_values(stream_key, dims, deviation, reach, pieces=(), kind=jnp.bfloat16):
    result = deviation * jax.random.normal(stream_key, dims, jnp.float32)
    if pieces:
        result = result * steps_of(stream_key, dims, pieces, -0.22, 0.18)
    return jnp.clip(result, -reach, reach).astype(kind)


def setup_inputs(seed: int = 0) -> dict:
    key_list = jax.random.split(jax.random.key(seed), 7)
    return {
        "hidden": normal_values(key_list[0], (Q, D), 1.0, 6.0, ((0, 4),)),
        "norm_gain": jnp.clip(1.0 + 0.1 * jax.random.normal(key_list[1], (D,), jnp.float32), 0.5, 1.5),
        "proj_weight": normal_values(key_list[2], (D, D), D ** -0.5, 0.09375, ((0, 8), (1, 4))),
        "pq_codes": place_ends(jax.random.randint(key_list[3], (PSG_TOTAL, M), 0, K), jax.random.fold_in(key_list[3], 1), 0, K - 1).astype(jnp.int32),
        "codebook": draw_codebook(jax.random.fold_in(key_list[6], 71), 0),
        "positives": place_ends(jax.random.randint(key_list[5], (Q,), 0, PSG_TOTAL), jax.random.fold_in(key_list[5], 1), 0, PSG_TOTAL - 1).astype(jnp.int32),
    }


score_scale = 0.0625
norm_eps = 1e-06

def reference(hidden, norm_gain, proj_weight, pq_codes, codebook, positives):
    floats_in = hidden.astype(jnp.float32)
    inverse = lax.rsqrt(lax.optimization_barrier(jnp.mean(floats_in * floats_in, axis=1, keepdims=True)) + norm_eps)
    normed = (floats_in * inverse * norm_gain[None, :]).astype(jnp.bfloat16)
    queries = jnp.dot(normed, proj_weight, preferred_element_type=jnp.float32).astype(jnp.bfloat16)
    code_table = jnp.transpose(codebook, (0, 2, 1))
    subspace = jnp.arange(M, dtype=jnp.int32)
    passages = code_table[subspace[None, :], pq_codes].reshape(pq_codes.shape[0], D)
    scores = lax.dot_general(queries, passages, (((1,), (1,)), ((), ())), preferred_element_type=jnp.float32) * score_scale
    row_max = lax.optimization_barrier(jnp.max(scores, axis=1, keepdims=True))
    expands = jnp.exp(scores - row_max)
    row_total = lax.optimization_barrier(jnp.sum(expands, axis=1, keepdims=True))
    target = jnp.arange(pq_codes.shape[0], dtype=jnp.int32)[None, :] == positives[:, None]
    positive_score = lax.optimization_barrier(jnp.sum(jnp.where(target, scores, 0.0), axis=1))
    losses = jnp.log(row_total[:, 0]) + row_max[:, 0] - positive_score
    score_grad = (expands / row_total - target.astype(jnp.float32)).astype(jnp.bfloat16)
    query_grad = (jnp.dot(score_grad, passages, preferred_element_type=jnp.float32) * score_scale).astype(jnp.bfloat16)
    passage_grad = (lax.dot_general(score_grad, queries, (((0,), (0,)), ((), ())), preferred_element_type=jnp.float32) * score_scale).astype(jnp.bfloat16)
    segment_ids = (subspace[None, :] * K + pq_codes).reshape(-1).astype(jnp.int32)
    flattened = passage_grad.astype(jnp.float32).reshape(-1, SUB)
    book_sum = jax.ops.segment_sum(flattened, segment_ids, num_segments=M * K)
    codebook_grad = jnp.transpose(book_sum.reshape(M, K, SUB), (0, 2, 1))
    weight_grad = lax.dot_general(normed, query_grad, (((0,), (0,)), ((), ())), preferred_element_type=jnp.float32)
    block_width = D // N_QRY
    norm_back = jnp.zeros((hidden.shape[0], D), jnp.float32)
    for column_group in range(N_QRY):
        low_edge = column_group * block_width
        product = lax.dot_general(query_grad[:, low_edge:low_edge + block_width], proj_weight[:, low_edge:low_edge + block_width], (((1,), (1,)), ((), ())), preferred_element_type=jnp.float32)
        norm_back = norm_back + lax.optimization_barrier(product.astype(jnp.bfloat16)).astype(jnp.float32)
    scaled = norm_back * norm_gain[None, :]
    hidden_grad = (inverse * scaled - floats_in * inverse * inverse * inverse * lax.optimization_barrier(jnp.mean(scaled * floats_in, axis=1, keepdims=True))).astype(jnp.bfloat16)
    return (losses, hidden_grad, weight_grad, codebook_grad)
```

```python
import functools

import jax
import jax.numpy as jnp
from jax import lax
from jax.experimental import pallas as pl
from jax.experimental.pallas import tpu as pltpu
from jax.sharding import PartitionSpec as P

score_scale = 0.0625
norm_eps = 1e-06
bf16 = jnp.bfloat16
f32 = jnp.float32


def whole(array):
    rank = len(array.shape)
    return pl.BlockSpec(array.shape, lambda *step: (0,) * rank)


def cost(flops, moved, exps=0):
    return pl.CostEstimate(flops=int(flops), bytes_accessed=int(moved), transcendentals=int(exps))


def part_body(order, stack, weight, part, rows):
    count, height = part.shape[0], part.shape[1]
    for k in range(count):
        rows[pl.ds(k * height, height), :] = stack[order[k]]
    full = jnp.dot(rows[...], weight[...], preferred_element_type=f32)
    part[...] = full.reshape(part.shape)


def query_part(order, stack, weight):
    count, height, depth = order.shape[0], stack.shape[1], stack.shape[2]
    columns = weight.shape[1]
    return pl.pallas_call(
        part_body,
        grid_spec=pltpu.PrefetchScalarGridSpec(
            num_scalar_prefetch=1,
            grid=(1,),
            in_specs=[whole(stack), whole(weight)],
            out_specs=[
                pl.BlockSpec((count, height, columns), lambda i, order: (0, 0, 0)),
                pl.BlockSpec((count * height, depth), lambda i, order: (0, 0)),
            ],
        ),
        out_shape=[
            jax.ShapeDtypeStruct((count, height, columns), f32),
            jax.ShapeDtypeStruct((count * height, depth), bf16),
        ],
        cost_estimate=cost(2 * count * height * depth * columns, weight.size * 2),
        name="query_part",
    )(order, stack, weight)


def decode_body(order, codes, table, out, index):
    count, width = codes.shape[1], codes.shape[2]
    index[...] = codes[0].astype(f32).astype(jnp.int32)
    for m in range(count):
        full = jnp.broadcast_to(index[m : m + 1, :], (8, width))
        low = full & 127
        high = full >= 128
        values = table[0, 0, pl.ds(m * 8, 8), :].astype(f32)
        first, second = values[:, :128], values[:, 128:]
        pieces = []
        for c in range(width // 128):
            lanes = slice(c * 128, (c + 1) * 128)
            a = jnp.take_along_axis(first, low[:, lanes], axis=1, mode="promise_in_bounds")
            b = jnp.take_along_axis(second, low[:, lanes], axis=1, mode="promise_in_bounds")
            pieces.append(jnp.where(high[:, lanes], b, a))
        out[pl.ds(m * 8, 8), :] = jnp.concatenate(pieces, axis=1).astype(bf16)


def decode(order, codes, tables, layer):
    slices, count, width = codes.shape
    height = count * 8
    return pl.pallas_call(
        decode_body,
        grid_spec=pltpu.PrefetchScalarGridSpec(
            num_scalar_prefetch=1,
            grid=(slices,),
            in_specs=[
                pl.BlockSpec((1, count, width), lambda i, order: (i, 0, 0)),
                pl.BlockSpec(
                    (1, 1, height, tables.shape[3]), lambda i, order: (order[i], layer, 0, 0)
                ),
            ],
            out_specs=pl.BlockSpec((height, width), lambda i, order: (i, 0)),
            scratch_shapes=[pltpu.VMEM((count, width), jnp.int32)],
        ),
        out_shape=jax.ShapeDtypeStruct((slices * height, width), bf16),
        cost_estimate=cost(4 * slices * height * width * 512, slices * height * width * 2),
        name="decode",
    )(order, codes, tables)


def score_body(chunks, blocks, *refs):
    queries, tables = refs[:chunks], refs[chunks : chunks + blocks]
    target, scores, stats, held = refs[chunks + blocks :]
    step, tile = pl.program_id(0), tables[0].shape[1]
    height = queries[0].shape[1]
    rows = scores.shape[0]

    @pl.when(step == 0)
    def gather():
        for c in range(chunks):
            for b in range(blocks):
                held[b, pl.ds(c * height, height), :] = queries[c][b]

    total = jnp.dot(held[0], tables[0][...], preferred_element_type=f32)
    for b in range(1, blocks):
        total += jnp.dot(held[b], tables[b][...], preferred_element_type=f32)
    scores[:, pl.ds(pl.multiple_of(step * tile, tile), tile)] = total * score_scale

    @pl.when(step == pl.num_programs(0) - 1)
    def reduce():
        group = 64
        for r in range(rows // group):
            span = pl.ds(r * group, group)
            value = scores[span, :]
            largest = jnp.max(value, axis=1, keepdims=True)
            expsum = jnp.sum(jnp.exp(value - largest), axis=1, keepdims=True)
            column = lax.broadcasted_iota(jnp.int32, value.shape, 1)
            hit = jnp.sum(
                jnp.where(column == target[span, :], value, 0.0), axis=1, keepdims=True
            )
            lane = lax.broadcasted_iota(jnp.int32, (group, 128), 1)
            packed = jnp.where(lane == 0, largest, jnp.where(lane == 1, expsum, hit))
            stats[span, :] = packed


def scores_of(queries, tables, target):
    chunks, blocks = len(queries), len(tables)
    _, height, depth = queries[0].shape
    width = tables[0].shape[1]
    rows, tile = chunks * height, min(512, width)
    return pl.pallas_call(
        functools.partial(score_body, chunks, blocks),
        grid=(width // tile,),
        in_specs=[whole(q) for q in queries]
        + [pl.BlockSpec((depth, tile), lambda i: (0, i)) for _ in tables]
        + [whole(target)],
        out_specs=[
            pl.BlockSpec((rows, width), lambda i: (0, 0)),
            pl.BlockSpec((rows, 128), lambda i: (0, 0)),
        ],
        out_shape=[
            jax.ShapeDtypeStruct((rows, width), f32),
            jax.ShapeDtypeStruct((rows, 128), f32),
        ],
        scratch_shapes=[pltpu.VMEM((blocks, rows, depth), bf16)],
        cost_estimate=cost(
            2 * rows * blocks * depth * width, blocks * depth * width * 2, rows * width
        ),
        name="scores",
    )(*queries, *tables, target)


def grad_body(scores, largest, total, target, passages, grad, part):
    step, tile = pl.program_id(0), scores.shape[1]
    column = lax.broadcasted_iota(jnp.int32, scores.shape, 1) + step * tile
    hit = (column == target[...]).astype(f32)
    value = (jnp.exp(scores[...] - largest[...]) / total[...] - hit).astype(bf16)
    grad[...] = value
    product = lax.dot_general(
        value, passages[...], (((1,), (1,)), ((), ())), preferred_element_type=f32
    )

    @pl.when(step == 0)
    def begin():
        part[...] = product

    @pl.when(step > 0)
    def add():
        part[...] += product

    @pl.when(step == pl.num_programs(0) - 1)
    def scale():
        part[...] = part[...] * score_scale


def score_grads(scores, largest, total, target, passages):
    rows, width = scores.shape
    depth, tile = passages.shape[0], min(512, width)
    return pl.pallas_call(
        grad_body,
        grid=(width // tile,),
        in_specs=[
            pl.BlockSpec((rows, tile), lambda i: (0, i)),
            whole(largest),
            whole(total),
            whole(target),
            pl.BlockSpec((depth, tile), lambda i: (0, i)),
        ],
        out_specs=[
            pl.BlockSpec((rows, tile), lambda i: (0, i)),
            pl.BlockSpec((rows, depth), lambda i: (0, 0)),
        ],
        out_shape=[
            jax.ShapeDtypeStruct((rows, width), bf16),
            jax.ShapeDtypeStruct((rows, depth), f32),
        ],
        cost_estimate=cost(2 * rows * width * depth, rows * width * 6, rows * width),
        name="score_grads",
    )(scores, largest, total, target, passages)


def book_body(chunks, low_count, group, *refs):
    queries = refs[: 2 * chunks]
    first, second, codes, out, low_codes, high_codes = refs[2 * chunks :]
    count, width = codes.shape[1], codes.shape[2]
    high_count = 256 // low_count
    contract = (((0,), (0,)), ((), ()))
    upper = jnp.concatenate([q[0] for q in queries[:chunks]], axis=0)
    lower = jnp.concatenate([q[0] for q in queries[chunks:]], axis=0)
    grads = lax.dot_general(upper, first[...], contract, preferred_element_type=f32)
    grads += lax.dot_general(lower, second[...], contract, preferred_element_type=f32)
    grads = (grads * score_scale).astype(bf16)
    code = codes[0].astype(f32)
    high = jnp.floor(code * (1.0 / low_count))
    high_codes[...] = high
    low_codes[...] = code - high * low_count
    low_iota = lax.broadcasted_iota(jnp.int32, (low_count, 128), 0).astype(f32).astype(bf16)
    high_iota = lax.broadcasted_iota(jnp.int32, (high_count * 8, 128), 0) // 8
    high_iota = high_iota.astype(f32).astype(bf16)
    low_iota = jnp.tile(low_iota, (1, width // 128))
    high_iota = jnp.tile(high_iota, (1, width // 128))
    one, zero = jnp.ones((), bf16), jnp.zeros((), bf16)
    for g in range(count // group):
        hots, masked = [], []
        for m in range(g * group, (g + 1) * group):
            low = jnp.broadcast_to(low_codes[m : m + 1, :].astype(bf16), (low_count, width))
            top = jnp.broadcast_to(high_codes[m : m + 1, :].astype(bf16), (high_count * 8, width))
            grad = jnp.tile(grads[m * 8 : (m + 1) * 8, :], (high_count, 1))
            hots.append(jnp.where(low == low_iota, one, zero))
            masked.append(jnp.where(top == high_iota, grad, zero))
        product = lax.dot_general(
            jnp.concatenate(masked, axis=0),
            jnp.concatenate(hots, axis=0),
            (((1,), (1,)), ((), ())),
            preferred_element_type=f32,
        )
        for i in range(group):
            height = high_count * 8
            block = product[i * height : (i + 1) * height, i * low_count : (i + 1) * low_count]
            out[g * group + i] = jnp.concatenate(
                [block[b * 8 : (b + 1) * 8, :] for b in range(high_count)], axis=1
            )


def book_grads(queries, grads, codes):
    chunks = len(queries) // 2
    height = queries[0].shape[1]
    slices, count, width = codes.shape
    span = count * 8
    return pl.pallas_call(
        functools.partial(book_body, chunks, 64, 4),
        grid=(slices,),
        in_specs=[pl.BlockSpec((1, height, span), lambda i: (0, 0, i)) for _ in queries]
        + [whole(g) for g in grads]
        + [pl.BlockSpec((1, count, width), lambda i: (i, 0, 0))],
        out_specs=pl.BlockSpec((count, 8, 256), lambda i: (i, 0, 0)),
        out_shape=jax.ShapeDtypeStruct((slices * count, 8, 256), f32),
        scratch_shapes=[pltpu.VMEM((count, width), f32), pltpu.VMEM((count, width), f32)],
        cost_estimate=cost(8 * slices * span * width * 512, slices * span * width * 2),
        name="book_grads",
    )(*queries, *grads, codes)


def back_body(chunks, *refs):
    pieces, weight, out, rows = refs[:chunks], refs[chunks], refs[chunks + 1], refs[chunks + 2]
    height = pieces[0].shape[0]
    for c in range(chunks):
        rows[pl.ds(c * height, height), :] = pieces[c][...]
    out[...] = lax.dot_general(
        rows[...], weight[...], (((1,), (1,)), ((), ())), preferred_element_type=f32
    ).astype(bf16)


def back_part(pieces, weight):
    height, depth = pieces[0].shape
    rows = height * len(pieces)
    return pl.pallas_call(
        functools.partial(back_body, len(pieces)),
        grid=(1,),
        in_specs=[whole(p) for p in pieces] + [whole(weight)],
        out_specs=[
            pl.BlockSpec((rows, weight.shape[0]), lambda i: (0, 0)),
            pl.BlockSpec((rows, depth), lambda i: (0, 0)),
        ],
        out_shape=[
            jax.ShapeDtypeStruct((rows, weight.shape[0]), bf16),
            jax.ShapeDtypeStruct((rows, depth), bf16),
        ],
        cost_estimate=cost(2 * rows * weight.size, rows * depth * 4),
        name="back_part",
    )(*pieces, weight)


def tail_body(chunks, order, *refs):
    pieces = refs[:chunks]
    hidden, gain, inverse, out = refs[chunks:]
    width = pieces[0].shape[1]
    dots = jnp.zeros((hidden.shape[0], 1), f32)
    for c in range(chunks):
        lanes = pl.ds(pl.multiple_of(order[c] * width, width), width)
        scaled = pieces[c][...] * gain[:, lanes]
        dots += jnp.sum(scaled * hidden[:, lanes].astype(f32), axis=1, keepdims=True)
    scale = inverse[...]
    mean = dots * (1.0 / (chunks * width))
    factor = scale * scale * scale * mean
    for c in range(chunks):
        lanes = pl.ds(pl.multiple_of(order[c] * width, width), width)
        scaled = pieces[c][...] * gain[:, lanes]
        out[:, lanes] = (scale * scaled - hidden[:, lanes].astype(f32) * factor).astype(bf16)


def hidden_tail(order, pieces, hidden, gain, inverse):
    return pl.pallas_call(
        functools.partial(tail_body, len(pieces)),
        grid_spec=pltpu.PrefetchScalarGridSpec(
            num_scalar_prefetch=1,
            grid=(1,),
            in_specs=[whole(p) for p in pieces] + [whole(hidden), whole(gain), whole(inverse)],
            out_specs=whole(hidden),
        ),
        out_shape=jax.ShapeDtypeStruct(hidden.shape, bf16),
        cost_estimate=cost(8 * hidden.size, hidden.size * 8),
        name="hidden_tail",
    )(order, *pieces, hidden, gain, inverse)


def reorder_body(order, source, out):
    out[...] = source[...]


def reorder(order, source):
    shape = source.shape
    rest = (0,) * (len(shape) - 1)
    return pl.pallas_call(
        reorder_body,
        grid_spec=pltpu.PrefetchScalarGridSpec(
            num_scalar_prefetch=1,
            grid=(shape[0],),
            in_specs=[pl.BlockSpec((1,) + shape[1:], lambda i, order: (order[i],) + rest)],
            out_specs=pl.BlockSpec((1,) + shape[1:], lambda i, order: (i,) + rest),
        ),
        out_shape=jax.ShapeDtypeStruct(shape, source.dtype),
        name="reorder",
    )(order, source)


def per_device(hidden, norm_gain, proj_weight, pq_codes, codebook, positives):
    shards, owners = lax.axis_size("psg"), lax.axis_size("qry")
    shard, owner = lax.axis_index("psg"), lax.axis_index("qry")
    half = shards // 2
    place = (shard % 2) * half + shard // 2
    steps = jnp.arange(shards, dtype=jnp.int32)
    swapped = steps ^ place

    def core(x):
        return lax.ppermute(x, "psg", [(i, i ^ 1) for i in range(shards)])

    def chip(x, k):
        return lax.ppermute(x, "psg", [(i, i ^ (2 * k)) for i in range(shards)])

    def turn(x, k):
        return lax.ppermute(x, "qry", [(i, (i + k) % owners) for i in range(owners)])

    def collect(x):
        near = [x] + [chip(x, k) for k in range(1, half)]
        return near, [core(piece) for piece in near]

    own_rows, features = hidden.shape
    row_span, columns = proj_weight.shape
    passage_count, sub_count = pq_codes.shape
    queries_all = own_rows * owners
    chunk = queries_all // shards
    per_owner = own_rows // chunk

    floats = hidden.astype(f32)
    inverse = lax.rsqrt(jnp.mean(floats * floats, axis=1, keepdims=True) + norm_eps)
    normed = (floats * inverse * norm_gain[None, :]).astype(bf16)
    slice_own = lax.dynamic_slice_in_dim(normed, shard * row_span, row_span, 1)
    slices = [slice_own] + [turn(slice_own, k) for k in range(1, owners)]
    stack = jnp.concatenate(slices, axis=0).reshape(shards, chunk, row_span)
    from_owner = (owner - swapped // per_owner) % owners
    where_in = from_owner * per_owner + swapped % per_owner

    book_rows = sub_count // shards
    codes_own = pq_codes.astype(bf16).T.reshape(shards, book_rows, passage_count)
    book_own = codebook.reshape(shards, 1, book_rows * 8, codebook.shape[2])
    book_slice = lax.dynamic_index_in_dim(book_own, place, 0, keepdims=False)
    book_slices = jnp.concatenate([turn(book_slice, k) for k in range(1, owners)], axis=0)
    near, far = collect(book_slices)
    books = jnp.stack(near + far)
    codes = [codes_own] + [turn(codes_own, k) for k in range(1, owners)]
    passages = [decode(steps, codes_own, book_own, 0)]
    for k in range(1, owners):
        passages.append(decode(swapped, codes[k], books, k - 1))

    far_part, far_rows = query_part(where_in[half:], stack, proj_weight)
    near_part, near_rows = query_part(where_in[:half], stack, proj_weight)

    def scatter_sum(near_term, far_term):
        summed = near_term + core(far_term)
        total = summed[0]
        for k in range(1, half):
            total = total + chip(summed[k], k)
        return total

    query_own = scatter_sum(near_part, far_part).astype(bf16)
    query_blocks = jnp.stack([query_own] + [turn(query_own, k) for k in range(1, owners)])
    near_queries, far_queries = collect(query_blocks)

    targets = positives.reshape(shards, chunk)[swapped].reshape(2, half * chunk, 1)
    targets = targets - shard * passage_count
    near_scores, near_stats = scores_of(near_queries, passages, targets[0])
    far_scores, far_stats = scores_of(far_queries, passages, targets[1])

    stats = jnp.stack([near_stats[:, :3].T, far_stats[:, :3].T], axis=1)
    stats = stats.reshape(3, 2, half, chunk)

    def merge(values):
        largest = functools.reduce(jnp.maximum, [v[0] for v in values])
        total = sum(v[1] * jnp.exp(v[0] - largest) for v in values)
        return jnp.stack([largest, total, sum(v[2] for v in values)])

    stats = merge([stats, core(stats)[:, ::-1]])
    others = []
    for k in range(1, half):
        other = chip(stats, k)
        others.append(jnp.stack([other[:, :, i ^ k] for i in range(half)], axis=2))
    stats = merge([stats] + others)
    row_max, row_total, positive_score = stats.reshape(3, 2, half * chunk, 1)
    losses_all = (jnp.log(row_total) + row_max - positive_score).reshape(-1)

    far_grad, far_term = score_grads(
        far_scores, row_max[1], row_total[1], targets[1], passages[0]
    )
    near_grad, near_term = score_grads(
        near_scores, row_max[0], row_total[0], targets[0], passages[0]
    )
    query_grad = scatter_sum(
        near_term.reshape(half, chunk, columns), far_term.reshape(half, chunk, columns)
    ).astype(bf16)
    near_pieces, far_pieces = collect(query_grad)

    group = min(sub_count, 16)
    book_part = book_grads(
        near_queries + far_queries,
        [near_grad, far_grad],
        codes_own.reshape(sub_count // group, group, passage_count),
    )
    book_part = reorder(swapped, book_part.reshape(shards, book_rows * 8, 256))
    book_half = book_part[:half] + core(book_part[half:])
    book_sum = book_half[0]
    for k in range(1, half):
        book_sum = book_sum + chip(book_half[k].astype(bf16), k).astype(f32)
    near_books, far_books = collect(book_sum)
    codebook_grad = reorder(swapped, jnp.stack(near_books + far_books)).reshape(codebook.shape)

    back, grad_rows = back_part(near_pieces + far_pieces, proj_weight)
    normed_rows = jnp.concatenate([near_rows, far_rows], axis=0)
    weight_grad = lax.dot_general(
        normed_rows, grad_rows, (((0,), (0,)), ((), ())), preferred_element_type=f32
    )

    def rows_of(array, who):
        first = (who ^ (place // per_owner)) * own_rows
        return lax.dynamic_slice_in_dim(array, first, own_rows, 0)

    def straighten(array):
        bit = 1
        while bit < per_owner:
            shaped = array.reshape((per_owner // (2 * bit), 2, bit * chunk) + array.shape[1:])
            turned = shaped[:, ::-1].reshape(array.shape)
            array = jnp.where((place // bit) % 2 == 1, turned, array)
            bit *= 2
        return array

    back_sum = rows_of(back, owner).astype(f32)
    for k in range(1, owners):
        back_sum = back_sum + turn(rows_of(back, (owner + k) % owners), k).astype(f32)
    back_sum = straighten(back_sum)
    near_back, far_back = collect(back_sum)
    shard_of = (swapped % half) * 2 + swapped // half
    hidden_grad = hidden_tail(
        shard_of, near_back + far_back, hidden, norm_gain[None, :], inverse
    )
    losses = straighten(rows_of(losses_all, owner))
    return (losses, hidden_grad, weight_grad, codebook_grad)


def solution(mesh):
    in_specs = (P("qry", None), P(), P("psg", "qry"), P("psg", "qry"), P("qry", None, None), P())
    out_specs = (P("qry"), P("qry", None), P("psg", "qry"), P("qry", None, None))
    return jax.shard_map(
        per_device, mesh=mesh, in_specs=in_specs, out_specs=out_specs, check_vma=False
    )
```

```python
import functools

import jax
import jax.numpy as jnp
from jax import lax
from jax.experimental import pallas as pl
from jax.experimental.pallas import tpu as pltpu
from jax.sharding import PartitionSpec as P


score_scale = 0.0625
norm_eps = 1e-06
bf16 = jnp.bfloat16
f32 = jnp.float32


def whole(array):
    rank = len(array.shape)
    return pl.BlockSpec(array.shape, lambda *step: (0,) * rank)


def cost(flops, moved, exps=0):
    return pl.CostEstimate(flops=int(flops), bytes_accessed=int(moved), transcendentals=int(exps))


def arrange_body(count, order, *refs):
    pieces, out = refs[:-1], refs[-1]
    for c, piece in enumerate(pieces):
        for i in range(count):
            out[order[c * count + i]] = piece[i].astype(out.dtype)


def arrange(order, pieces, kind=None):
    count = pieces[0].shape[0]
    shape = (count * len(pieces),) + pieces[0].shape[1:]
    rank = len(shape)
    return pl.pallas_call(
        functools.partial(arrange_body, count),
        grid_spec=pltpu.PrefetchScalarGridSpec(
            num_scalar_prefetch=1,
            grid=(1,),
            in_specs=[whole(p) for p in pieces],
            out_specs=pl.BlockSpec(shape, lambda i, order: (0,) * rank),
        ),
        out_shape=jax.ShapeDtypeStruct(shape, kind or pieces[0].dtype),
        cost_estimate=cost(0, 8 * len(pieces) * pieces[0].size),
        name="arrange",
    )(order, *pieces)


def decode_body(*refs):
    parts, table, out, index = refs[:-3], refs[-3], refs[-2], refs[-1]
    count, width = index.shape
    index[...] = sum(codes[0].astype(f32) for codes in parts).astype(jnp.int32)
    for m in range(count):
        full = jnp.broadcast_to(index[m : m + 1, :], (8, width))
        low = full & 127
        high = full >= 128
        values = table[0, pl.ds(m * 8, 8), :].astype(f32)
        first, second = values[:, :128], values[:, 128:]
        pieces = []
        for c in range(width // 128):
            lanes = slice(c * 128, (c + 1) * 128)
            a = jnp.take_along_axis(first, low[:, lanes], axis=1, mode="promise_in_bounds")
            b = jnp.take_along_axis(second, low[:, lanes], axis=1, mode="promise_in_bounds")
            pieces.append(jnp.where(high[:, lanes], b, a))
        out[pl.ds(m * 8, 8), :] = jnp.concatenate(pieces, axis=1).astype(bf16)


def decode(parts, tables, layer):
    slices, count, width = parts[0].shape
    height = count * 8
    return pl.pallas_call(
        decode_body,
        grid=(slices,),
        in_specs=[
            pl.BlockSpec((1, count, width), lambda i: (i, 0, 0)) for _ in parts
        ]
        + [pl.BlockSpec((1, height, tables.shape[2]), lambda i: (i, layer, 0))],
        out_specs=pl.BlockSpec((height, width), lambda i: (i, 0)),
        scratch_shapes=[pltpu.VMEM((count, width), jnp.int32)],
        out_shape=jax.ShapeDtypeStruct((slices * height, width), bf16),
        cost_estimate=cost(4 * slices * height * width * 512, slices * height * width * 2),
        name="decode",
    )(*parts, tables)


def score_body(chunks, blocks, *refs):
    queries, tables = refs[:chunks], refs[chunks : chunks + blocks]
    target, scores, stats, held = refs[chunks + blocks :]
    step, tile = pl.program_id(0), tables[0].shape[1]
    height = queries[0].shape[1]
    rows = scores.shape[0]

    @pl.when(step == 0)
    def gather():
        for c in range(chunks):
            for b in range(blocks):
                held[b, pl.ds(c * height, height), :] = queries[c][b]

    total = jnp.dot(held[0], tables[0][...], preferred_element_type=f32)
    for b in range(1, blocks):
        total += jnp.dot(held[b], tables[b][...], preferred_element_type=f32)
    scores[:, pl.ds(pl.multiple_of(step * tile, tile), tile)] = total * score_scale

    @pl.when(step == pl.num_programs(0) - 1)
    def reduce():
        group = 128
        for r in range(rows // group):
            span = pl.ds(r * group, group)
            value = scores[span, :]
            largest = jnp.max(value, axis=1, keepdims=True)
            expsum = jnp.sum(jnp.exp(value - largest), axis=1, keepdims=True)
            column = lax.broadcasted_iota(jnp.int32, value.shape, 1)
            hit = jnp.sum(
                jnp.where(column == target[span, :], value, 0.0), axis=1, keepdims=True
            )
            lane = lax.broadcasted_iota(jnp.int32, (group, 128), 1)
            packed = jnp.where(lane == 0, largest, jnp.where(lane == 1, expsum, hit))
            stats[:, span] = packed.T[:8]


def scores_of(queries, tables, target):
    chunks, blocks = len(queries), len(tables)
    _, height, depth = queries[0].shape
    width = tables[0].shape[1]
    rows, tile = chunks * height, min(512, width)
    return pl.pallas_call(
        functools.partial(score_body, chunks, blocks),
        grid=(width // tile,),
        in_specs=[whole(q) for q in queries]
        + [pl.BlockSpec((depth, tile), lambda i: (0, i)) for _ in tables]
        + [whole(target)],
        out_specs=[
            pl.BlockSpec((rows, width), lambda i: (0, 0)),
            pl.BlockSpec((8, rows), lambda i: (0, 0)),
        ],
        out_shape=[
            jax.ShapeDtypeStruct((rows, width), f32),
            jax.ShapeDtypeStruct((8, rows), f32),
        ],
        scratch_shapes=[pltpu.VMEM((blocks, rows, depth), bf16)],
        cost_estimate=cost(
            2 * rows * blocks * depth * width, blocks * depth * width * 2, rows * width
        ),
        name="scores",
    )(*queries, *tables, target)


def shuffle(value, offset, chunk):
    count = value.shape[1] // chunk
    return jnp.concatenate(
        [value[:, (c ^ offset) * chunk : ((c ^ offset) + 1) * chunk] for c in range(count)], axis=1
    )


def grad_body(shards, *refs):
    stats = refs[:shards]
    scores, target, passages, grad, near, far, losses, largest, total = refs[shards:]
    step, tile = pl.program_id(0), scores.shape[1]
    rows = scores.shape[0]

    @pl.when(step == 0)
    def merge():
        values = [shuffle(s[...], c, rows // shards) for c, s in enumerate(stats)]
        most = functools.reduce(jnp.maximum, [v[0:1] for v in values])
        summed = sum(v[1:2] * jnp.exp(v[0:1] - most) for v in values)
        hits = sum(v[2:3] for v in values)
        losses[...] = jnp.broadcast_to(jnp.log(summed) + most - hits, losses.shape)
        largest[...] = jnp.broadcast_to(most, (128, rows)).T
        total[...] = jnp.broadcast_to(summed, (128, rows)).T
        near[...] = jnp.zeros_like(near)
        far[...] = jnp.zeros_like(far)

    group = 128
    for r in range(rows // group):
        span = pl.ds(r * group, group)
        shifted = scores[span, :] - jnp.tile(largest[span, :], (1, tile // 128))
        column = lax.broadcasted_iota(jnp.int32, (group, tile), 1) + step * tile
        hit = (column == target[span, :]).astype(f32)
        value = jnp.exp(shifted) / jnp.tile(total[span, :], (1, tile // 128)) - hit
        grad[span, :] = value.astype(bf16)
    term = score_scale * lax.dot_general(
        grad[...], passages[...], (((1,), (1,)), ((), ())), preferred_element_type=f32
    )
    near[...] += term[: rows // 2].reshape(near.shape)
    far[...] += term[rows // 2 :].reshape(far.shape)


def score_grads(scores, stats, target, passages):
    rows, width = scores.shape
    depth, tile = passages.shape[0], min(512, width)
    term = (len(stats) // 2, rows // len(stats), depth)
    return pl.pallas_call(
        functools.partial(grad_body, len(stats)),
        grid=(width // tile,),
        in_specs=[whole(s) for s in stats]
        + [
            pl.BlockSpec((rows, tile), lambda i: (0, i)),
            whole(target),
            pl.BlockSpec((depth, tile), lambda i: (0, i)),
        ],
        out_specs=[
            pl.BlockSpec((rows, tile), lambda i: (0, i)),
            pl.BlockSpec(term, lambda i: (0, 0, 0)),
            pl.BlockSpec(term, lambda i: (0, 0, 0)),
            pl.BlockSpec((8, rows), lambda i: (0, 0)),
        ],
        out_shape=[
            jax.ShapeDtypeStruct((rows, width), bf16),
            jax.ShapeDtypeStruct(term, f32),
            jax.ShapeDtypeStruct(term, f32),
            jax.ShapeDtypeStruct((8, rows), f32),
        ],
        scratch_shapes=[pltpu.VMEM((rows, 128), f32), pltpu.VMEM((rows, 128), f32)],
        cost_estimate=cost(2 * rows * width * depth, rows * width * 6, rows * width),
        name="score_grads",
    )(*stats, scores, target, passages)


def book_body(chunks, low_count, group, order, *refs):
    queries = refs[:chunks]
    score_grad, codes, out, low_codes, high_codes = refs[chunks:]
    count, width = codes.shape[1], codes.shape[2]
    high_count = 256 // low_count
    contract = (((0,), (0,)), ((), ()))
    rows = jnp.concatenate([q[0] for q in queries], axis=0)
    grads = lax.dot_general(rows, score_grad[...], contract, preferred_element_type=f32)
    grads = (grads * score_scale).astype(bf16)
    code = codes[0].astype(f32)
    high = jnp.floor(code * (1.0 / low_count))
    high_codes[...] = high
    low_codes[...] = code - high * low_count
    low_iota = lax.broadcasted_iota(jnp.int32, (low_count, 128), 0).astype(f32).astype(bf16)
    high_iota = lax.broadcasted_iota(jnp.int32, (high_count * 8, 128), 0) // 8
    high_iota = high_iota.astype(f32).astype(bf16)
    low_iota = jnp.tile(low_iota, (1, width // 128))
    high_iota = jnp.tile(high_iota, (1, width // 128))
    one, zero = jnp.ones((), bf16), jnp.zeros((), bf16)
    for g in range(count // group):
        hots, masked = [], []
        for m in range(g * group, (g + 1) * group):
            low = jnp.broadcast_to(low_codes[m : m + 1, :].astype(bf16), (low_count, width))
            top = jnp.broadcast_to(high_codes[m : m + 1, :].astype(bf16), (high_count * 8, width))
            grad = jnp.tile(grads[m * 8 : (m + 1) * 8, :], (high_count, 1))
            hots.append(jnp.where(low == low_iota, one, zero))
            masked.append(jnp.where(top == high_iota, grad, zero))
        product = lax.dot_general(
            jnp.concatenate(masked, axis=0),
            jnp.concatenate(hots, axis=0),
            (((1,), (1,)), ((), ())),
            preferred_element_type=f32,
        )
        for i in range(group):
            height = high_count * 8
            block = product[i * height : (i + 1) * height, i * low_count : (i + 1) * low_count]
            out[g * group + i] = jnp.concatenate(
                [block[b * 8 : (b + 1) * 8, :] for b in range(high_count)], axis=1
            )


def book_grads(order, queries, score_grad, codes):
    chunks = len(queries)
    height = queries[0].shape[1]
    count, width = codes.shape[1:]
    slices, span = order.shape[0], count * 8
    return pl.pallas_call(
        functools.partial(book_body, chunks, 64, 4),
        grid_spec=pltpu.PrefetchScalarGridSpec(
            num_scalar_prefetch=1,
            grid=(slices,),
            in_specs=[
                pl.BlockSpec((1, height, span), lambda i, order: (0, 0, order[i])) for _ in queries
            ]
            + [
                pl.BlockSpec(score_grad.shape, lambda i, order: (0, 0)),
                pl.BlockSpec((1, count, width), lambda i, order: (order[i], 0, 0)),
            ],
            out_specs=pl.BlockSpec((count, 8, 256), lambda i, order: (i, 0, 0)),
            scratch_shapes=[pltpu.VMEM((count, width), f32), pltpu.VMEM((count, width), f32)],
        ),
        out_shape=jax.ShapeDtypeStruct((slices * count, 8, 256), f32),
        cost_estimate=cost(8 * slices * span * width * 512, slices * span * width * 2),
        name="book_grads",
    )(order, *queries, score_grad, codes)


def back_body(chunks, owners, order, *refs):
    pieces, weight = refs[:chunks], refs[chunks]
    outs, rows, sorted_rows = refs[chunks + 1 : -2], refs[-2], refs[-1]
    height = pieces[0].shape[0]
    for c in range(chunks):
        rows[pl.ds(c * height, height), :] = pieces[c][...]
        sorted_rows[order[c]] = pieces[c][...]
    span = rows.shape[0] // owners
    result = lax.dot_general(
        sorted_rows[...].reshape(rows.shape),
        weight[...],
        (((1,), (1,)), ((), ())),
        preferred_element_type=f32,
    ).astype(bf16)
    for k in range(owners):
        outs[k][...] = result[k * span : (k + 1) * span]


def back_part(order, pieces, weight, owners):
    height, depth = pieces[0].shape
    rows, width = height * len(pieces), weight.shape[0]
    blocks = [jax.ShapeDtypeStruct((rows // owners, width), bf16)] * owners
    return pl.pallas_call(
        functools.partial(back_body, len(pieces), owners),
        grid_spec=pltpu.PrefetchScalarGridSpec(
            num_scalar_prefetch=1,
            grid=(1,),
            in_specs=[whole(p) for p in pieces] + [whole(weight)],
            out_specs=[whole(b) for b in blocks]
            + [pl.BlockSpec((rows, depth), lambda i, order: (0, 0))],
            scratch_shapes=[pltpu.VMEM((len(pieces), height, depth), bf16)],
        ),
        out_shape=blocks + [jax.ShapeDtypeStruct((rows, depth), bf16)],
        cost_estimate=cost(2 * rows * weight.size, rows * depth * 4),
        name="back_part",
    )(order, *pieces, weight)


def tail_body(chunks, order, *refs):
    pieces = refs[:chunks]
    hidden, gain, inverse, out = refs[chunks:]
    width = pieces[0].shape[1]
    dots = jnp.zeros((hidden.shape[0], 1), f32)
    for c in range(chunks):
        lanes = pl.ds(pl.multiple_of(order[c] * width, width), width)
        scaled = pieces[c][...] * gain[:, lanes]
        dots += jnp.sum(scaled * hidden[:, lanes].astype(f32), axis=1, keepdims=True)
    scale = inverse[...]
    mean = dots * (1.0 / (chunks * width))
    factor = scale * scale * scale * mean
    for c in range(chunks):
        lanes = pl.ds(pl.multiple_of(order[c] * width, width), width)
        scaled = pieces[c][...] * gain[:, lanes]
        out[:, lanes] = (scale * scaled - hidden[:, lanes].astype(f32) * factor).astype(bf16)


def hidden_tail(order, pieces, hidden, gain, inverse):
    rows, features = hidden.shape
    height = rows
    by_rows = lambda i, order: (i, 0)
    return pl.pallas_call(
        functools.partial(tail_body, len(pieces)),
        grid_spec=pltpu.PrefetchScalarGridSpec(
            num_scalar_prefetch=1,
            grid=(rows // height,),
            in_specs=[pl.BlockSpec((height, p.shape[1]), by_rows) for p in pieces]
            + [
                pl.BlockSpec((height, features), by_rows),
                whole(gain),
                pl.BlockSpec((height, 1), by_rows),
            ],
            out_specs=pl.BlockSpec((height, features), by_rows),
        ),
        out_shape=jax.ShapeDtypeStruct(hidden.shape, bf16),
        cost_estimate=cost(8 * hidden.size, hidden.size * 8),
        name="hidden_tail",
    )(order, *pieces, hidden, gain, inverse)


def run_device(hidden, norm_gain, proj_weight, pq_codes, codebook, positives):
    shards, owners = lax.axis_size("psg"), lax.axis_size("qry")
    shard, owner = lax.axis_index("psg"), lax.axis_index("qry")
    half = shards // 2
    place = (shard % 2) * half + shard // 2
    steps = jnp.arange(shards, dtype=jnp.int32)
    swapped = steps ^ place

    def core(x):
        return lax.ppermute(x, "psg", [(i, i ^ 1) for i in range(shards)])

    def chip(x, k):
        return lax.ppermute(x, "psg", [(i, i ^ (2 * k)) for i in range(shards)])

    def turn(x, k):
        return lax.ppermute(x, "qry", [(i, i ^ k) for i in range(owners)])

    def collect(x):
        near = [x] + [chip(x, k) for k in range(1, half)]
        return near, [core(piece) for piece in near]

    def after(value, *others):
        return lax.optimization_barrier((value,) + others)[0]

    own_rows, _ = hidden.shape
    row_span, columns = proj_weight.shape
    passage_count, sub_count = pq_codes.shape
    queries_all = own_rows * owners
    chunk = queries_all // shards
    per_owner = own_rows // chunk

    book_rows = sub_count // shards
    book_own = codebook.reshape(shards, book_rows * 8, codebook.shape[2])
    book_slice = lax.dynamic_slice_in_dim(book_own, place, 1, 0)
    book_slices = jnp.concatenate([turn(book_slice, k) for k in range(1, owners)], axis=1)
    near, far = collect(book_slices)
    books = arrange(swapped, near + far)

    floats = hidden.astype(f32)
    inverse = lax.rsqrt(jnp.mean(floats * floats, axis=1, keepdims=True) + norm_eps)
    first = shard * row_span
    part = lax.dynamic_slice_in_dim(hidden, first, row_span, 1).astype(f32)
    part_gain = lax.dynamic_slice_in_dim(norm_gain, first, row_span, 0)
    slice_own = (part * inverse * part_gain[None, :]).astype(bf16)
    slices = [slice_own] + [turn(slice_own, k) for k in range(1, owners)]
    codes_own = pq_codes.astype(bf16).T.reshape(shards, book_rows, passage_count)
    source = after(owner ^ (steps // per_owner), codes_own)
    goes_to = (source * per_owner + steps % per_owner) ^ place
    normed_rows = arrange(goes_to, [s.reshape(per_owner, chunk, row_span) for s in slices])
    normed_rows = normed_rows.reshape(queries_all, row_span)

    def term_of(rows):
        return jnp.dot(rows, proj_weight, preferred_element_type=f32).reshape(half, chunk, columns)

    def scatter_sum(near_term, far_term):
        arrived = core(far_term)
        summed = [near_term[k] + arrived[k] for k in range(half)]
        total = summed[0]
        for k in range(1, half):
            total = total + chip(summed[k], k)
        return total, summed

    far_part = term_of(normed_rows[half * chunk :])
    near_part = after(term_of(normed_rows[: half * chunk]))
    query_own, _ = scatter_sum(near_part, far_part)
    query_own = query_own.astype(bf16)
    first_passages = decode([codes_own], book_own, 0)

    turned = [turn(query_own, k) for k in range(1, owners)]
    query_blocks = jnp.stack([query_own] + turned)
    near_queries, far_queries = collect(query_blocks)

    def hop(x, pairs):
        return lax.ppermute(x, "qry", pairs)

    passages = [first_passages]
    codes = {}
    waiting = after(codes_own, query_blocks)
    for k in range(1, owners):
        if owners == 4 and k == 3:
            passed = after(codes[2][0], query_blocks)
            codes[k] = [hop(waiting, [(1, 2), (2, 1)]), hop(passed, [(1, 0), (2, 3)])]
        else:
            codes[k] = [turn(codes_own if k <= owners // 2 else waiting, k)]
        passages.append(decode(codes[k], books, k - 1))

    targets = positives.reshape(shards, chunk)[swapped].reshape(queries_all, 1)
    targets = targets - shard * passage_count
    query_chunks = near_queries + far_queries
    scores, stats = scores_of(query_chunks, passages, targets)
    near_stats, far_stats = collect(stats)
    score_grad, near_term, far_term, losses_all = score_grads(
        scores, near_stats + far_stats, targets, passages[0]
    )
    query_grad, grad_sums = scatter_sum(near_term, far_term)
    near_pieces, far_pieces = collect(query_grad.astype(bf16))

    def book_terms(order):
        grads = after(score_grad, grad_sums[-1])
        if book_rows % 16 == 0:
            return book_grads(order, query_chunks, grads, codes_own).reshape(
                order.shape[0], book_rows * 8, 256
            )
        group = min(sub_count, 16)
        grouped = codes_own.reshape(sub_count // group, group, passage_count)
        book = book_grads(steps[: sub_count // group], query_chunks, grads, grouped)
        return book.reshape(shards, book_rows * 8, 256)[order]

    far_book = core(book_terms(swapped[half:]))
    first_book = book_terms(swapped[1:half])

    dest = ((swapped // per_owner) ^ owner) * per_owner + swapped % per_owner
    *back, grad_rows = back_part(dest, near_pieces + far_pieces, proj_weight, owners)
    weight_grad = lax.dot_general(
        normed_rows, grad_rows, (((0,), (0,)), ((), ())), preferred_element_type=f32
    )
    second_book = book_terms(swapped[:1])
    book_sum = second_book[0] + far_book[0]
    for k in range(1, half):
        book_half = (first_book[k - 1] + far_book[k]).astype(bf16)
        book_sum = book_sum + chip(book_half, k).astype(f32)
    near_books, far_books = collect(book_sum[None].astype(bf16))
    codebook_grad = arrange(swapped, near_books + far_books, f32).reshape(codebook.shape)

    def rows_of(array, who):
        first = (who ^ (place // per_owner)) * own_rows
        return lax.dynamic_slice_in_dim(array, first, own_rows, 0)

    def straighten(array):
        bit = 1
        while bit < per_owner:
            shaped = array.reshape(per_owner // (2 * bit), 2, bit * chunk)
            turned = shaped[:, ::-1].reshape(array.shape)
            array = jnp.where((place // bit) % 2 == 1, turned, array)
            bit *= 2
        return array

    back_sum = back[0].astype(f32)
    for k in range(1, owners):
        back_sum = back_sum + turn(back[k], k).astype(f32)
    near_back, far_back = collect(back_sum)
    shard_of = (swapped % half) * 2 + swapped // half
    hidden_grad = hidden_tail(
        shard_of, near_back + far_back, hidden, norm_gain[None, :], inverse
    )
    losses = straighten(rows_of(losses_all[0], owner))
    return (losses, hidden_grad, weight_grad, codebook_grad)


def solution(mesh):
    in_specs = (P("qry", None), P(), P("psg", "qry"), P("psg", "qry"), P("qry", None, None), P())
    out_specs = (P("qry"), P("qry", None), P("psg", "qry"), P("qry", None, None))
    return jax.shard_map(
        run_device, mesh=mesh, in_specs=in_specs, out_specs=out_specs, check_vma=False
    )
```

```python
import functools

import jax
import jax.numpy as jnp
from jax import lax
from jax.experimental import pallas as pl
from jax.experimental.pallas import tpu as pltpu
from jax.sharding import PartitionSpec as P


score_scale = 0.0625
norm_eps = 1e-06
bf16 = jnp.bfloat16
f32 = jnp.float32


def whole(array):
    rank = len(array.shape)
    return pl.BlockSpec(array.shape, lambda *step: (0,) * rank)


def cost(flops, moved, exps=0):
    return pl.CostEstimate(flops=int(flops), bytes_accessed=int(moved), transcendentals=int(exps))


def tree(values, join=lambda a, b: a + b):
    while len(values) > 1:
        values = [join(values[i], values[i + 1]) for i in range(0, len(values), 2)]
    return values[0]


def arrange_body(count, order, *refs):
    pieces, out = refs[:-1], refs[-1]
    for c, piece in enumerate(pieces):
        for i in range(count):
            out[order[c * count + i]] = piece[i].astype(out.dtype)


def arrange(order, pieces, kind=None):
    count = pieces[0].shape[0]
    shape = (count * len(pieces),) + pieces[0].shape[1:]
    rank = len(shape)
    return pl.pallas_call(
        functools.partial(arrange_body, count),
        grid_spec=pltpu.PrefetchScalarGridSpec(
            num_scalar_prefetch=1,
            grid=(1,),
            in_specs=[whole(p) for p in pieces],
            out_specs=pl.BlockSpec(shape, lambda i, order: (0,) * rank),
        ),
        out_shape=jax.ShapeDtypeStruct(shape, kind or pieces[0].dtype),
        cost_estimate=cost(0, 8 * len(pieces) * pieces[0].size),
        name="arrange",
    )(order, *pieces)


def decode_body(*refs):
    parts, table, out, index = refs[:-3], refs[-3], refs[-2], refs[-1]
    pair, count, width = index.shape
    index[...] = sum(codes[...].astype(f32) for codes in parts).astype(jnp.int32)
    for j, m in [(j, m) for j in range(pair) for m in range(count)]:
        full = jnp.broadcast_to(index[j, m : m + 1, :], (8, width))
        low = full & 127
        high = full >= 128
        values = table[j, pl.ds(m * 8, 8), :].astype(f32)
        first, second = values[:, :128], values[:, 128:]
        pieces = []
        for c in range(width // 128):
            lanes = slice(c * 128, (c + 1) * 128)
            a = jnp.take_along_axis(first, low[:, lanes], axis=1, mode="promise_in_bounds")
            b = jnp.take_along_axis(second, low[:, lanes], axis=1, mode="promise_in_bounds")
            pieces.append(jnp.where(high[:, lanes], b, a))
        out[pl.ds((j * count + m) * 8, 8), :] = jnp.concatenate(pieces, axis=1).astype(bf16)


def decode(parts, tables, layer):
    slices, count, width = parts[0].shape
    height = count * 8
    return pl.pallas_call(
        decode_body,
        grid=(slices // 2,),
        in_specs=[pl.BlockSpec((2, count, width), lambda i: (i, 0, 0)) for _ in parts]
        + [pl.BlockSpec((2, height, tables.shape[2]), lambda i: (i, layer, 0))],
        out_specs=pl.BlockSpec((2 * height, width), lambda i: (i, 0)),
        scratch_shapes=[pltpu.VMEM((2, count, width), jnp.int32)],
        out_shape=jax.ShapeDtypeStruct((slices * height, width), bf16),
        cost_estimate=cost(4 * slices * height * width * 512, slices * height * width * 2),
        name="decode",
    )(*parts, tables)


def column_of(row):
    return jnp.broadcast_to(row, (128, row.shape[1])).T


def score_body(chunks, blocks, *refs):
    own, others = refs[:chunks], refs[chunks : 2 * chunks]
    tables = refs[2 * chunks : 2 * chunks + blocks]
    target, scores, stats, own_rows, held, places, packed = refs[2 * chunks + blocks :]
    step, last = pl.program_id(0), pl.num_programs(0) - 1
    tile = tables[0].shape[1]
    height = own[0].shape[0]
    rows = scores.shape[0]
    group = 128

    @pl.when(step == 0)
    def gather():
        for c in range(chunks):
            own_rows[pl.ds(c * height, height), :] = own[c][...]
            held[0, pl.ds(c * height, height), :] = own[c][...]
            for b in range(1, blocks):
                held[b, pl.ds(c * height, height), :] = others[c][b - 1]
        places[...] = column_of(target[...])
        packed[...] = jnp.zeros_like(packed)

    def multiply():
        total = jnp.dot(held[0], tables[0][...], preferred_element_type=f32)
        for b in range(1, blocks):
            total += jnp.dot(held[b], tables[b][...], preferred_element_type=f32)
        scores[:, pl.ds(pl.multiple_of(step * tile, tile), tile)] = total * score_scale

    def reduce(t):
        column = lax.broadcasted_iota(jnp.int32, (group, tile), 1) + t * tile
        column = column.astype(f32)
        lane = lax.broadcasted_iota(jnp.int32, (group, 128), 1) - 3 * t
        for r in range(rows // group):
            span = pl.ds(r * group, group)
            value = scores[span, pl.ds(pl.multiple_of(t * tile, tile), tile)]
            largest = jnp.max(value, axis=1, keepdims=True)
            expsum = jnp.sum(jnp.exp(value - largest), axis=1, keepdims=True)
            found = column == jnp.tile(places[span, :], (1, tile // 128))
            hit = jnp.sum(jnp.where(found, value, 0.0), axis=1, keepdims=True)
            row = jnp.where(lane == 1, expsum, jnp.where(lane == 2, hit, packed[span, :]))
            packed[span, :] = jnp.where(lane == 0, largest, row)

    @pl.when(step == 0)
    def begin():
        multiply()

    @pl.when((step > 0) & (step < last))
    def both():
        reduce(step - 1)
        multiply()

    @pl.when(step == last)
    def finish():
        reduce(last - 1)
        tiles = scores.shape[1] // tile
        for r in range(rows // group):
            span = pl.ds(r * group, group)
            turned = packed[span, :].T
            most = functools.reduce(
                jnp.maximum, [turned[3 * t : 3 * t + 1] for t in range(tiles)]
            )
            total = sum(
                turned[3 * t + 1 : 3 * t + 2] * jnp.exp(turned[3 * t : 3 * t + 1] - most)
                for t in range(tiles)
            )
            hits = sum(turned[3 * t + 2 : 3 * t + 3] for t in range(tiles))
            stats[:, span] = jnp.concatenate(
                [most, total, hits, jnp.zeros((5, group), f32)], axis=0
            )


def scores_of(own, queries, tables, target):
    chunks, blocks = len(queries), len(tables)
    height, depth = own[0].shape
    width = tables[0].shape[1]
    rows, tile = chunks * height, min(512, width)
    return pl.pallas_call(
        functools.partial(score_body, chunks, blocks),
        grid=(width // tile + 1,),
        in_specs=[whole(q) for q in own + queries]
        + [pl.BlockSpec((depth, tile), lambda i: (0, jnp.minimum(i, width // tile - 1))) for _ in tables]
        + [whole(target)],
        out_specs=[
            pl.BlockSpec((rows, width), lambda i: (0, 0)),
            pl.BlockSpec((8, rows), lambda i: (0, 0)),
            pl.BlockSpec((rows, depth), lambda i: (0, 0)),
        ],
        out_shape=[
            jax.ShapeDtypeStruct((rows, width), f32),
            jax.ShapeDtypeStruct((8, rows), f32),
            jax.ShapeDtypeStruct((rows, depth), bf16),
        ],
        scratch_shapes=[
            pltpu.VMEM((blocks, rows, depth), bf16),
            pltpu.VMEM((rows, 128), f32),
            pltpu.VMEM((rows, 128), f32),
        ],
        cost_estimate=cost(
            2 * rows * blocks * depth * width, blocks * depth * width * 2, rows * width
        ),
        name="scores",
    )(*own, *queries, *tables, target)


def shuffle(value, offset, chunk):
    count = value.shape[1] // chunk
    return jnp.concatenate(
        [value[:, (c ^ offset) * chunk : ((c ^ offset) + 1) * chunk] for c in range(count)], axis=1
    )


def grad_body(shards, *refs):
    stats = refs[:shards]
    scores, target, passages, grad, near, far, losses = refs[shards:-3]
    largest, total, places = refs[-3:]
    step, tile = pl.program_id(0), scores.shape[1]
    rows = scores.shape[0]

    @pl.when(step == 0)
    def merge():
        values = [shuffle(s[...], c, rows // shards) for c, s in enumerate(stats)]
        most = tree([v[0:1] for v in values], jnp.maximum)
        summed = tree([v[1:2] * jnp.exp(v[0:1] - most) for v in values])
        hits = tree([v[2:3] for v in values])
        losses[...] = jnp.broadcast_to(jnp.log(summed) + most - hits, losses.shape)
        largest[...] = column_of(most)
        total[...] = column_of(1.0 / summed)
        places[...] = column_of(target[...])
        near[...] = jnp.zeros_like(near)
        far[...] = jnp.zeros_like(far)

    group = 128
    for r in range(rows // group):
        span = pl.ds(r * group, group)
        shifted = scores[span, :] - jnp.tile(largest[span, :], (1, tile // 128))
        column = (lax.broadcasted_iota(jnp.int32, (group, tile), 1) + step * tile).astype(f32)
        hit = (column == jnp.tile(places[span, :], (1, tile // 128))).astype(f32)
        value = jnp.exp(shifted) * jnp.tile(total[span, :], (1, tile // 128)) - hit
        grad[span, :] = value.astype(bf16)
    term = score_scale * lax.dot_general(
        grad[...], passages[...], (((1,), (1,)), ((), ())), preferred_element_type=f32
    )
    near[...] += term[: rows // 2].reshape(near.shape)
    far[...] += term[rows // 2 :].reshape(far.shape)


def score_grads(scores, stats, target, passages):
    rows, width = scores.shape
    depth, tile = passages.shape[0], min(512, width)
    term = (len(stats) // 2, rows // len(stats), depth)
    return pl.pallas_call(
        functools.partial(grad_body, len(stats)),
        grid=(width // tile,),
        in_specs=[whole(s) for s in stats]
        + [
            pl.BlockSpec((rows, tile), lambda i: (0, i)),
            whole(target),
            pl.BlockSpec((depth, tile), lambda i: (0, i)),
        ],
        out_specs=[
            pl.BlockSpec((rows, tile), lambda i: (0, i)),
            pl.BlockSpec(term, lambda i: (0, 0, 0)),
            pl.BlockSpec(term, lambda i: (0, 0, 0)),
            pl.BlockSpec((8, rows), lambda i: (0, 0)),
        ],
        out_shape=[
            jax.ShapeDtypeStruct((rows, width), bf16),
            jax.ShapeDtypeStruct(term, f32),
            jax.ShapeDtypeStruct(term, f32),
            jax.ShapeDtypeStruct((8, rows), f32),
        ],
        scratch_shapes=[pltpu.VMEM((rows, 128), f32)] * 3,
        cost_estimate=cost(2 * rows * width * depth, rows * width * 6, rows * width),
        name="score_grads",
    )(*stats, scores, target, passages)


def book_body(low_count, group, order, grads, codes, out, low_codes, high_codes):
    count, width = codes.shape[1], codes.shape[2]
    high_count = 256 // low_count
    code = codes[0].astype(f32)
    high = jnp.floor(code * (1.0 / low_count))
    high_codes[...] = high
    low_codes[...] = code - high * low_count
    low_iota = lax.broadcasted_iota(jnp.int32, (low_count, 128), 0).astype(f32).astype(bf16)
    high_iota = lax.broadcasted_iota(jnp.int32, (high_count * 8, 128), 0) // 8
    high_iota = high_iota.astype(f32).astype(bf16)
    low_iota = jnp.tile(low_iota, (1, width // 128))
    high_iota = jnp.tile(high_iota, (1, width // 128))
    one, zero = jnp.ones((), bf16), jnp.zeros((), bf16)
    for g in range(count // group):
        hots, masked = [], []
        for m in range(g * group, (g + 1) * group):
            low = jnp.broadcast_to(low_codes[m : m + 1, :].astype(bf16), (low_count, width))
            top = jnp.broadcast_to(high_codes[m : m + 1, :].astype(bf16), (high_count * 8, width))
            grad = jnp.tile(grads[pl.ds(m * 8, 8), :], (high_count, 1))
            hots.append(jnp.where(low == low_iota, one, zero))
            masked.append(jnp.where(top == high_iota, grad, zero))
        product = lax.dot_general(
            jnp.concatenate(masked, axis=0),
            jnp.concatenate(hots, axis=0),
            (((1,), (1,)), ((), ())),
            preferred_element_type=f32,
        )
        for i in range(group):
            height = high_count * 8
            block = product[i * height : (i + 1) * height, i * low_count : (i + 1) * low_count]
            out[g * group + i] = jnp.concatenate(
                [block[b * 8 : (b + 1) * 8, :] for b in range(high_count)], axis=1
            )


def book_grads(order, grads, codes):
    count, width = codes.shape[1:]
    slices, span = order.shape[0], count * 8
    return pl.pallas_call(
        functools.partial(book_body, 32, 4),
        grid_spec=pltpu.PrefetchScalarGridSpec(
            num_scalar_prefetch=1,
            grid=(slices,),
            in_specs=[
                pl.BlockSpec((span, width), lambda i, order: (order[i], 0)),
                pl.BlockSpec((1, count, width), lambda i, order: (order[i], 0, 0)),
            ],
            out_specs=pl.BlockSpec((count, 8, 256), lambda i, order: (i, 0, 0)),
            scratch_shapes=[pltpu.VMEM((count, width), f32), pltpu.VMEM((count, width), f32)],
        ),
        out_shape=jax.ShapeDtypeStruct((slices * count, 8, 256), f32),
        cost_estimate=cost(4 * slices * span * width * 512, slices * span * width * 2),
        name="book_grads",
    )(order, grads, codes)


def back_body(chunks, owners, order, *refs):
    pieces, weight = refs[:chunks], refs[chunks]
    outs, rows, sorted_rows = refs[chunks + 1 : -2], refs[-2], refs[-1]
    height = pieces[0].shape[0]
    for c in range(chunks):
        rows[pl.ds(c * height, height), :] = pieces[c][...]
        sorted_rows[order[c]] = pieces[c][...]
    span = rows.shape[0] // owners
    result = lax.dot_general(
        sorted_rows[...].reshape(rows.shape),
        weight[...],
        (((1,), (1,)), ((), ())),
        preferred_element_type=f32,
    ).astype(bf16)
    for k in range(owners):
        outs[k][...] = result[k * span : (k + 1) * span]


def back_part(order, pieces, weight, owners):
    height, depth = pieces[0].shape
    rows, width = height * len(pieces), weight.shape[0]
    blocks = [jax.ShapeDtypeStruct((rows // owners, width), bf16)] * owners
    return pl.pallas_call(
        functools.partial(back_body, len(pieces), owners),
        grid_spec=pltpu.PrefetchScalarGridSpec(
            num_scalar_prefetch=1,
            grid=(1,),
            in_specs=[whole(p) for p in pieces] + [whole(weight)],
            out_specs=[whole(b) for b in blocks]
            + [pl.BlockSpec((rows, depth), lambda i, order: (0, 0))],
            scratch_shapes=[pltpu.VMEM((len(pieces), height, depth), bf16)],
        ),
        out_shape=blocks + [jax.ShapeDtypeStruct((rows, depth), bf16)],
        cost_estimate=cost(2 * rows * weight.size, rows * depth * 4),
        name="back_part",
    )(order, *pieces, weight)


def tail_body(chunks, order, places, *refs):
    pieces, books = refs[:chunks], refs[chunks : 2 * chunks]
    hidden, gain, out, book_out = refs[2 * chunks :]
    for c in range(chunks):
        book_out[places[c]] = books[c][...].astype(f32)
    width = pieces[0].shape[1]
    dots, squares = [], []
    for c in range(chunks):
        lanes = pl.ds(pl.multiple_of(order[c] * width, width), width)
        value = hidden[:, lanes].astype(f32)
        scaled = pieces[c][...].astype(f32) * gain[:, lanes]
        dots.append(jnp.sum(scaled * value, axis=1, keepdims=True))
        squares.append(jnp.sum(value * value, axis=1, keepdims=True))
    count = chunks * width
    scale = lax.rsqrt(tree(squares) / count + norm_eps)
    factor = scale * scale * scale * (tree(dots) / count)
    for c in range(chunks):
        lanes = pl.ds(pl.multiple_of(order[c] * width, width), width)
        scaled = pieces[c][...].astype(f32) * gain[:, lanes]
        out[:, lanes] = (scale * scaled - hidden[:, lanes].astype(f32) * factor).astype(bf16)


def tail(order, places, pieces, books, width, book_shape, hidden, gain):
    shared = books is None
    rows = hidden.shape[0]
    book_rows, levels = book_shape
    here = width // levels if shared else 0
    book_spec = pl.BlockSpec((book_rows, levels), lambda i, order, places: (0, here))
    piece_spec = pl.BlockSpec((rows, width), lambda i, order, places: (0, 0))
    count = len(pieces)
    out_books = jax.ShapeDtypeStruct((count, book_rows, levels), f32)
    return pl.pallas_call(
        functools.partial(tail_body, count),
        grid_spec=pltpu.PrefetchScalarGridSpec(
            num_scalar_prefetch=2,
            grid=(1,),
            in_specs=[piece_spec] * count + [book_spec] * count + [whole(hidden), whole(gain)],
            out_specs=[whole(hidden), whole(out_books)],
        ),
        out_shape=[jax.ShapeDtypeStruct(hidden.shape, bf16), out_books],
        cost_estimate=cost(8 * hidden.size, hidden.size * 8),
        name="tail",
    )(order, places, *pieces, *(pieces if shared else books), hidden, gain)


def run_device(hidden, norm_gain, proj_weight, pq_codes, codebook, positives):
    shards, owners = lax.axis_size("psg"), lax.axis_size("qry")
    shard, owner = lax.axis_index("psg"), lax.axis_index("qry")
    half = shards // 2
    place = (shard % 2) * half + shard // 2
    steps = jnp.arange(shards, dtype=jnp.int32)
    swapped = steps ^ place

    def core(x):
        return lax.ppermute(x, "psg", [(i, i ^ 1) for i in range(shards)])

    def chip(x, k):
        return lax.ppermute(x, "psg", [(i, i ^ (2 * k)) for i in range(shards)])

    def turn(x, k):
        return lax.ppermute(x, "qry", [(i, i ^ k) for i in range(owners)])

    def collect(x):
        near = [x] + [chip(x, k) for k in range(1, half)]
        return near, [core(piece) for piece in near]

    def after(value, *others):
        return lax.optimization_barrier((value,) + others)[0]

    own_rows, _ = hidden.shape
    row_span, columns = proj_weight.shape
    passage_count, sub_count = pq_codes.shape
    queries_all = own_rows * owners
    chunk = queries_all // shards
    per_owner = own_rows // chunk

    book_rows = sub_count // shards
    book_own = codebook.reshape(shards, book_rows * 8, codebook.shape[2])
    book_slice = lax.dynamic_slice_in_dim(book_own, place, 1, 0)
    book_slices = jnp.concatenate([turn(book_slice, k) for k in range(1, owners)], axis=1)
    near, far = collect(book_slices)
    books = arrange(swapped, near + far)

    floats = hidden.astype(f32)
    inverse = lax.rsqrt(jnp.mean(floats * floats, axis=1, keepdims=True) + norm_eps)
    first = shard * row_span
    part = lax.dynamic_slice_in_dim(hidden, first, row_span, 1).astype(f32)
    part_gain = lax.dynamic_slice_in_dim(norm_gain, first, row_span, 0)
    slice_own = (part * inverse * part_gain[None, :]).astype(bf16)
    slices = [slice_own] + [turn(slice_own, k) for k in range(1, owners)]
    codes_own = pq_codes.astype(bf16).T.reshape(shards, book_rows, passage_count)
    targets = positives.reshape(shards, chunk)[swapped].reshape(1, queries_all)
    targets = (targets - shard * passage_count).astype(f32)
    source = after(owner ^ (steps // per_owner), codes_own, targets)
    goes_to = (source * per_owner + steps % per_owner) ^ place
    normed_rows = arrange(goes_to, [s.reshape(per_owner, chunk, row_span) for s in slices])
    normed_rows = normed_rows.reshape(queries_all, row_span)

    def term_of(rows):
        return jnp.dot(rows, proj_weight, preferred_element_type=f32).reshape(half, chunk, columns)

    def scatter_sum(near_term, far_term):
        arrived = core(far_term)
        summed = [near_term[k] + arrived[k] for k in range(half)]
        total = summed[0]
        for k in range(1, half):
            total = total + chip(summed[k], k)
        return total, summed

    far_part = term_of(normed_rows[half * chunk :])
    near_part = after(term_of(normed_rows[: half * chunk]))
    query_own, _ = scatter_sum(near_part, far_part)
    query_own = query_own.astype(bf16)
    first_passages = decode([codes_own], book_own, 0)

    query_blocks = jnp.stack([turn(query_own, k) for k in range(1, owners)])
    near_own, far_own = collect(query_own)
    near_queries, far_queries = collect(query_blocks)
    own_chunks = near_own + far_own

    def hop(x, pairs):
        return lax.ppermute(x, "qry", pairs)

    passages = [first_passages]
    codes = {}
    waiting = after(codes_own, query_blocks)
    for k in range(1, owners):
        if owners == 4 and k == 3:
            passed = after(codes[2][0], query_blocks)
            codes[k] = [hop(waiting, [(1, 2), (2, 1)]), hop(passed, [(1, 0), (2, 3)])]
        else:
            codes[k] = [turn(codes_own if k <= owners // 2 else waiting, k)]
        passages.append(decode(codes[k], books, k - 1))

    query_chunks = near_queries + far_queries
    scores, stats, own_rows_all = scores_of(own_chunks, query_chunks, passages, targets)
    near_stats, far_stats = collect(stats)
    score_grad, near_term, far_term, losses_all = score_grads(
        scores, near_stats + far_stats, targets, passages[0]
    )
    query_grad, grad_sums = scatter_sum(near_term, far_term)
    near_pieces, far_pieces = collect(query_grad.astype(bf16))

    passage_grad = lax.dot_general(
        own_rows_all,
        after(score_grad, grad_sums[-1]),
        (((0,), (0,)), ((), ())),
        preferred_element_type=f32,
    )
    passage_grad = (passage_grad * score_scale).astype(bf16)

    def book_of(order):
        if book_rows % 16 == 0:
            return book_grads(order, passage_grad, codes_own).reshape(
                order.shape[0], book_rows * 8, 256
            )
        group = min(sub_count, 16)
        grouped = codes_own.reshape(sub_count // group, group, passage_count)
        book = book_grads(steps[: sub_count // group], passage_grad, grouped)
        return book.reshape(shards, book_rows * 8, 256)[order]

    part = half // 2
    far_book = [core(book_of(swapped[half : half + part]))]
    both = book_of(jnp.concatenate([swapped[half + part :], swapped[part:half]]))
    far_book.append(core(both[:part]))
    near_book = [book_of(swapped[:part]), both[part:]]
    halves = [near_book[k // part][k % part] + far_book[k // part][k % part] for k in range(half)]
    book_sum = halves[0]
    for k in range(1, half):
        book_sum = book_sum + chip(halves[k].astype(bf16), k).astype(f32)
    book_sum = book_sum.astype(bf16)

    dest = ((swapped // per_owner) ^ owner) * per_owner + swapped % per_owner
    *back, grad_rows = back_part(dest, near_pieces + far_pieces, proj_weight, owners)
    weight_grad = lax.dot_general(
        normed_rows, grad_rows, (((0,), (0,)), ((), ())), preferred_element_type=f32
    )

    def rows_of(array, who):
        first = (who ^ (place // per_owner)) * own_rows
        return lax.dynamic_slice_in_dim(array, first, own_rows, 0)

    def straighten(array):
        bit = 1
        while bit < per_owner:
            shaped = array.reshape(per_owner // (2 * bit), 2, bit * chunk)
            turned = shaped[:, ::-1].reshape(array.shape)
            array = jnp.where((place // bit) % 2 == 1, turned, array)
            bit *= 2
        return array

    back_sum = back[0].astype(f32)
    for k in range(1, owners):
        back_sum = back_sum + turn(back[k], k).astype(f32)
    back_sum = back_sum.astype(bf16)
    book_shape = book_sum.shape
    shared = book_shape[0] == own_rows and row_span % book_shape[1] == 0
    books_last = None
    if shared:
        near_back, far_back = collect(jnp.concatenate([back_sum, book_sum], axis=1))
    else:
        near_back, far_back = collect(back_sum)
        books_last = sum(collect(book_sum), [])
    shard_of = (swapped % half) * 2 + swapped // half
    hidden_grad, codebook_grad = tail(
        shard_of,
        swapped,
        near_back + far_back,
        books_last,
        row_span,
        book_shape,
        hidden,
        norm_gain[None, :],
    )
    codebook_grad = codebook_grad.reshape(codebook.shape)
    losses = straighten(rows_of(losses_all[0], owner))
    return (losses, hidden_grad, weight_grad, codebook_grad)


def solution(mesh):
    in_specs = (P("qry", None), P(), P("psg", "qry"), P("psg", "qry"), P("qry", None, None), P())
    out_specs = (P("qry"), P("qry", None), P("psg", "qry"), P("qry", None, None))
    return jax.shard_map(
        run_device, mesh=mesh, in_specs=in_specs, out_specs=out_specs, check_vma=False
    )
```

```python
import functools

import jax
import jax.numpy as jnp
from jax import lax
from jax.experimental import pallas as pl
from jax.experimental.pallas import tpu as pltpu
from jax.sharding import PartitionSpec as P


score_scale = 0.0625
norm_eps = 1e-06
bf16 = jnp.bfloat16
f32 = jnp.float32


def whole(array):
    rank = len(array.shape)
    return pl.BlockSpec(array.shape, lambda *step: (0,) * rank)


def cost(flops, moved, exps=0):
    return pl.CostEstimate(flops=int(flops), bytes_accessed=int(moved), transcendentals=int(exps))


def tree(values, join=lambda a, b: a + b):
    while len(values) > 1:
        values = [join(values[i], values[i + 1]) for i in range(0, len(values), 2)]
    return values[0]


def arrange_body(count, order, *refs):
    pieces, out = refs[:-1], refs[-1]
    for c, piece in enumerate(pieces):
        for i in range(count):
            out[order[c * count + i]] = piece[i].astype(out.dtype)


def arrange(order, pieces, kind=None):
    count = pieces[0].shape[0]
    shape = (count * len(pieces),) + pieces[0].shape[1:]
    rank = len(shape)
    return pl.pallas_call(
        functools.partial(arrange_body, count),
        grid_spec=pltpu.PrefetchScalarGridSpec(
            num_scalar_prefetch=1,
            grid=(1,),
            in_specs=[whole(p) for p in pieces],
            out_specs=pl.BlockSpec(shape, lambda i, order: (0,) * rank),
        ),
        out_shape=jax.ShapeDtypeStruct(shape, kind or pieces[0].dtype),
        cost_estimate=cost(0, 8 * len(pieces) * pieces[0].size),
        name="arrange",
    )(order, *pieces)


def decode_body(*refs):
    parts, table, out, index = refs[:-3], refs[-3], refs[-2], refs[-1]
    pair, count, width = index.shape
    index[...] = sum(codes[...].astype(f32) for codes in parts).astype(jnp.int32)
    for j, m in [(j, m) for j in range(pair) for m in range(count)]:
        full = jnp.broadcast_to(index[j, m : m + 1, :], (8, width))
        low = full & 127
        high = full >= 128
        values = table[j, pl.ds(m * 8, 8), :].astype(f32)
        first, second = values[:, :128], values[:, 128:]
        pieces = []
        for c in range(width // 128):
            lanes = slice(c * 128, (c + 1) * 128)
            a = jnp.take_along_axis(first, low[:, lanes], axis=1, mode="promise_in_bounds")
            b = jnp.take_along_axis(second, low[:, lanes], axis=1, mode="promise_in_bounds")
            pieces.append(jnp.where(high[:, lanes], b, a))
        out[pl.ds((j * count + m) * 8, 8), :] = jnp.concatenate(pieces, axis=1).astype(bf16)


def decode(parts, tables, layer):
    slices, count, width = parts[0].shape
    height = count * 8
    return pl.pallas_call(
        decode_body,
        grid=(slices // 2,),
        in_specs=[pl.BlockSpec((2, count, width), lambda i: (i, 0, 0)) for _ in parts]
        + [pl.BlockSpec((2, height, tables.shape[2]), lambda i: (i, layer, 0))],
        out_specs=pl.BlockSpec((2 * height, width), lambda i: (i, 0)),
        scratch_shapes=[pltpu.VMEM((2, count, width), jnp.int32)],
        out_shape=jax.ShapeDtypeStruct((slices * height, width), bf16),
        cost_estimate=cost(4 * slices * height * width * 512, slices * height * width * 2),
        name="decode",
    )(*parts, tables)


def column_of(row):
    return jnp.broadcast_to(row, (128, row.shape[1])).T


def score_body(chunks, blocks, *refs):
    own, others = refs[:chunks], refs[chunks : 2 * chunks]
    tables = refs[2 * chunks : 2 * chunks + blocks]
    target, scores, stats, own_rows, held, places, packed = refs[2 * chunks + blocks :]
    step, last = pl.program_id(0), pl.num_programs(0) - 1
    tile = tables[0].shape[1]
    height = own[0].shape[0]
    rows = scores.shape[0]
    group = 128

    @pl.when(step == 0)
    def gather():
        for c in range(chunks):
            own_rows[pl.ds(c * height, height), :] = own[c][...]
            held[0, pl.ds(c * height, height), :] = own[c][...]
            for b in range(1, blocks):
                held[b, pl.ds(c * height, height), :] = others[c][b - 1]
        places[...] = column_of(target[...])
        packed[...] = jnp.zeros_like(packed)

    def multiply():
        total = jnp.dot(held[0], tables[0][...], preferred_element_type=f32)
        for b in range(1, blocks):
            total += jnp.dot(held[b], tables[b][...], preferred_element_type=f32)
        scores[:, pl.ds(pl.multiple_of(step * tile, tile), tile)] = total * score_scale

    def reduce(t):
        column = lax.broadcasted_iota(jnp.int32, (group, tile), 1) + t * tile
        column = column.astype(f32)
        lane = lax.broadcasted_iota(jnp.int32, (group, 128), 1) - 3 * t
        for r in range(rows // group):
            span = pl.ds(r * group, group)
            value = scores[span, pl.ds(pl.multiple_of(t * tile, tile), tile)]
            largest = jnp.max(value, axis=1, keepdims=True)
            expsum = jnp.sum(jnp.exp(value - largest), axis=1, keepdims=True)
            found = column == jnp.tile(places[span, :], (1, tile // 128))
            hit = jnp.sum(jnp.where(found, value, 0.0), axis=1, keepdims=True)
            row = jnp.where(lane == 1, expsum, jnp.where(lane == 2, hit, packed[span, :]))
            packed[span, :] = jnp.where(lane == 0, largest, row)

    @pl.when(step == 0)
    def begin():
        multiply()

    @pl.when((step > 0) & (step < last))
    def both():
        reduce(step - 1)
        multiply()

    @pl.when(step == last)
    def finish():
        reduce(last - 1)
        tiles = scores.shape[1] // tile
        for r in range(rows // group):
            span = pl.ds(r * group, group)
            turned = packed[span, :].T
            most = functools.reduce(
                jnp.maximum, [turned[3 * t : 3 * t + 1] for t in range(tiles)]
            )
            total = sum(
                turned[3 * t + 1 : 3 * t + 2] * jnp.exp(turned[3 * t : 3 * t + 1] - most)
                for t in range(tiles)
            )
            hits = sum(turned[3 * t + 2 : 3 * t + 3] for t in range(tiles))
            stats[:, span] = jnp.concatenate(
                [most, total, hits, jnp.zeros((5, group), f32)], axis=0
            )


def scores_of(own, queries, tables, target):
    chunks, blocks = len(queries), len(tables)
    height, depth = own[0].shape
    width = tables[0].shape[1]
    rows, tile = chunks * height, min(512, width)
    return pl.pallas_call(
        functools.partial(score_body, chunks, blocks),
        grid=(width // tile + 1,),
        in_specs=[whole(q) for q in own + queries]
        + [pl.BlockSpec((depth, tile), lambda i: (0, jnp.minimum(i, width // tile - 1))) for _ in tables]
        + [whole(target)],
        out_specs=[
            pl.BlockSpec((rows, width), lambda i: (0, 0)),
            pl.BlockSpec((8, rows), lambda i: (0, 0)),
            pl.BlockSpec((rows, depth), lambda i: (0, 0)),
        ],
        out_shape=[
            jax.ShapeDtypeStruct((rows, width), f32),
            jax.ShapeDtypeStruct((8, rows), f32),
            jax.ShapeDtypeStruct((rows, depth), bf16),
        ],
        scratch_shapes=[
            pltpu.VMEM((blocks, rows, depth), bf16),
            pltpu.VMEM((rows, 128), f32),
            pltpu.VMEM((rows, 128), f32),
        ],
        cost_estimate=cost(
            2 * rows * blocks * depth * width, blocks * depth * width * 2, rows * width
        ),
        name="scores",
    )(*own, *queries, *tables, target)


def shuffle(value, offset, chunk):
    count = value.shape[1] // chunk
    return jnp.concatenate(
        [value[:, (c ^ offset) * chunk : ((c ^ offset) + 1) * chunk] for c in range(count)], axis=1
    )


def grad_body(shards, *refs):
    stats = refs[:shards]
    scores, target, passages, grad, near, far, losses = refs[shards:-3]
    largest, total, places = refs[-3:]
    step, tile = pl.program_id(0), scores.shape[1]
    rows = scores.shape[0]

    @pl.when(step == 0)
    def merge():
        values = [shuffle(s[...], c, rows // shards) for c, s in enumerate(stats)]
        most = tree([v[0:1] for v in values], jnp.maximum)
        summed = tree([v[1:2] * jnp.exp(v[0:1] - most) for v in values])
        hits = tree([v[2:3] for v in values])
        losses[...] = jnp.broadcast_to(jnp.log(summed) + most - hits, losses.shape)
        largest[...] = column_of(most)
        total[...] = column_of(1.0 / summed)
        places[...] = column_of(target[...])
        near[...] = jnp.zeros_like(near)
        far[...] = jnp.zeros_like(far)

    group = 128
    for r in range(rows // group):
        span = pl.ds(r * group, group)
        shifted = scores[span, :] - jnp.tile(largest[span, :], (1, tile // 128))
        column = (lax.broadcasted_iota(jnp.int32, (group, tile), 1) + step * tile).astype(f32)
        hit = (column == jnp.tile(places[span, :], (1, tile // 128))).astype(f32)
        value = jnp.exp(shifted) * jnp.tile(total[span, :], (1, tile // 128)) - hit
        grad[span, :] = value.astype(bf16)
    term = score_scale * lax.dot_general(
        grad[...], passages[...], (((1,), (1,)), ((), ())), preferred_element_type=f32
    )
    near[...] += term[: rows // 2].reshape(near.shape)
    far[...] += term[rows // 2 :].reshape(far.shape)


def score_grads(scores, stats, target, passages):
    rows, width = scores.shape
    depth, tile = passages.shape[0], min(512, width)
    term = (len(stats) // 2, rows // len(stats), depth)
    return pl.pallas_call(
        functools.partial(grad_body, len(stats)),
        grid=(width // tile,),
        in_specs=[whole(s) for s in stats]
        + [
            pl.BlockSpec((rows, tile), lambda i: (0, i)),
            whole(target),
            pl.BlockSpec((depth, tile), lambda i: (0, i)),
        ],
        out_specs=[
            pl.BlockSpec((rows, tile), lambda i: (0, i)),
            pl.BlockSpec(term, lambda i: (0, 0, 0)),
            pl.BlockSpec(term, lambda i: (0, 0, 0)),
            pl.BlockSpec((8, rows), lambda i: (0, 0)),
        ],
        out_shape=[
            jax.ShapeDtypeStruct((rows, width), bf16),
            jax.ShapeDtypeStruct(term, f32),
            jax.ShapeDtypeStruct(term, f32),
            jax.ShapeDtypeStruct((8, rows), f32),
        ],
        scratch_shapes=[pltpu.VMEM((rows, 128), f32)] * 3,
        cost_estimate=cost(2 * rows * width * depth, rows * width * 6, rows * width),
        name="score_grads",
    )(*stats, scores, target, passages)


def book_body(low_count, group, order, grads, codes, out, low_codes, high_codes):
    count, width = codes.shape[1], codes.shape[2]
    high_count = 256 // low_count
    code = codes[0].astype(f32)
    high = jnp.floor(code * (1.0 / low_count))
    high_codes[...] = high
    low_codes[...] = code - high * low_count
    low_iota = lax.broadcasted_iota(jnp.int32, (low_count, 128), 0).astype(f32).astype(bf16)
    high_iota = lax.broadcasted_iota(jnp.int32, (high_count * 8, 128), 0) // 8
    high_iota = high_iota.astype(f32).astype(bf16)
    low_iota = jnp.tile(low_iota, (1, width // 128))
    high_iota = jnp.tile(high_iota, (1, width // 128))
    one, zero = jnp.ones((), bf16), jnp.zeros((), bf16)
    for g in range(count // group):
        hots, masked = [], []
        for m in range(g * group, (g + 1) * group):
            low = jnp.broadcast_to(low_codes[m : m + 1, :].astype(bf16), (low_count, width))
            top = jnp.broadcast_to(high_codes[m : m + 1, :].astype(bf16), (high_count * 8, width))
            grad = jnp.tile(grads[pl.ds(m * 8, 8), :], (high_count, 1))
            hots.append(jnp.where(low == low_iota, one, zero))
            masked.append(jnp.where(top == high_iota, grad, zero))
        product = lax.dot_general(
            jnp.concatenate(masked, axis=0),
            jnp.concatenate(hots, axis=0),
            (((1,), (1,)), ((), ())),
            preferred_element_type=f32,
        )
        for i in range(group):
            height = high_count * 8
            block = product[i * height : (i + 1) * height, i * low_count : (i + 1) * low_count]
            out[g * group + i] = jnp.concatenate(
                [block[b * 8 : (b + 1) * 8, :] for b in range(high_count)], axis=1
            )


def book_grads(order, grads, codes):
    count, width = codes.shape[1:]
    slices, span = order.shape[0], count * 8
    return pl.pallas_call(
        functools.partial(book_body, 32, 4),
        grid_spec=pltpu.PrefetchScalarGridSpec(
            num_scalar_prefetch=1,
            grid=(slices,),
            in_specs=[
                pl.BlockSpec((span, width), lambda i, order: (order[i], 0)),
                pl.BlockSpec((1, count, width), lambda i, order: (order[i], 0, 0)),
            ],
            out_specs=pl.BlockSpec((count, 8, 256), lambda i, order: (i, 0, 0)),
            scratch_shapes=[pltpu.VMEM((count, width), f32), pltpu.VMEM((count, width), f32)],
        ),
        out_shape=jax.ShapeDtypeStruct((slices * count, 8, 256), f32),
        cost_estimate=cost(4 * slices * span * width * 512, slices * span * width * 2),
        name="book_grads",
    )(order, grads, codes)


def back_body(chunks, owners, order, *refs):
    pieces, weight = refs[:chunks], refs[chunks]
    outs, rows, sorted_rows = refs[chunks + 1 : -2], refs[-2], refs[-1]
    height = pieces[0].shape[0]
    for c in range(chunks):
        rows[pl.ds(c * height, height), :] = pieces[c][...]
        sorted_rows[order[c]] = pieces[c][...]
    span = rows.shape[0] // owners
    result = lax.dot_general(
        sorted_rows[...].reshape(rows.shape),
        weight[...],
        (((1,), (1,)), ((), ())),
        preferred_element_type=f32,
    ).astype(bf16)
    for k in range(owners):
        outs[k][...] = result[k * span : (k + 1) * span]


def back_part(order, pieces, weight, owners):
    height, depth = pieces[0].shape
    rows, width = height * len(pieces), weight.shape[0]
    blocks = [jax.ShapeDtypeStruct((rows // owners, width), bf16)] * owners
    return pl.pallas_call(
        functools.partial(back_body, len(pieces), owners),
        grid_spec=pltpu.PrefetchScalarGridSpec(
            num_scalar_prefetch=1,
            grid=(1,),
            in_specs=[whole(p) for p in pieces] + [whole(weight)],
            out_specs=[whole(b) for b in blocks]
            + [pl.BlockSpec((rows, depth), lambda i, order: (0, 0))],
            scratch_shapes=[pltpu.VMEM((len(pieces), height, depth), bf16)],
        ),
        out_shape=blocks + [jax.ShapeDtypeStruct((rows, depth), bf16)],
        cost_estimate=cost(2 * rows * weight.size, rows * depth * 4),
        name="back_part",
    )(order, *pieces, weight)


def tail_body(chunks, order, places, *refs):
    pieces, books = refs[:chunks], refs[chunks : 2 * chunks]
    hidden, gain, out, book_out = refs[2 * chunks :]
    for c in range(chunks):
        book_out[places[c]] = books[c][...].astype(f32)
    width = pieces[0].shape[1]
    dots, squares = [], []
    for c in range(chunks):
        lanes = pl.ds(pl.multiple_of(order[c] * width, width), width)
        value = hidden[:, lanes].astype(f32)
        scaled = pieces[c][...].astype(f32) * gain[:, lanes]
        dots.append(jnp.sum(scaled * value, axis=1, keepdims=True))
        squares.append(jnp.sum(value * value, axis=1, keepdims=True))
    count = chunks * width
    scale = lax.rsqrt(tree(squares) / count + norm_eps)
    factor = scale * scale * scale * (tree(dots) / count)
    for c in range(chunks):
        lanes = pl.ds(pl.multiple_of(order[c] * width, width), width)
        scaled = pieces[c][...].astype(f32) * gain[:, lanes]
        out[:, lanes] = (scale * scaled - hidden[:, lanes].astype(f32) * factor).astype(bf16)


def tail(order, places, pieces, books, width, book_shape, hidden, gain):
    shared = books is None
    rows = hidden.shape[0]
    book_rows, levels = book_shape
    here = width // levels if shared else 0
    book_spec = pl.BlockSpec((book_rows, levels), lambda i, order, places: (0, here))
    piece_spec = pl.BlockSpec((rows, width), lambda i, order, places: (0, 0))
    count = len(pieces)
    out_books = jax.ShapeDtypeStruct((count, book_rows, levels), f32)
    return pl.pallas_call(
        functools.partial(tail_body, count),
        grid_spec=pltpu.PrefetchScalarGridSpec(
            num_scalar_prefetch=2,
            grid=(1,),
            in_specs=[piece_spec] * count + [book_spec] * count + [whole(hidden), whole(gain)],
            out_specs=[whole(hidden), whole(out_books)],
        ),
        out_shape=[jax.ShapeDtypeStruct(hidden.shape, bf16), out_books],
        cost_estimate=cost(8 * hidden.size, hidden.size * 8),
        name="tail",
    )(order, places, *pieces, *(pieces if shared else books), hidden, gain)


def run_device(hidden, norm_gain, proj_weight, pq_codes, codebook, positives):
    shards, owners = lax.axis_size("psg"), lax.axis_size("qry")
    shard, owner = lax.axis_index("psg"), lax.axis_index("qry")
    half = shards // 2
    place = (shard % 2) * half + shard // 2
    steps = jnp.arange(shards, dtype=jnp.int32)
    swapped = steps ^ place

    def core(x):
        return lax.ppermute(x, "psg", [(i, i ^ 1) for i in range(shards)])

    def chip(x, k):
        return lax.ppermute(x, "psg", [(i, i ^ (2 * k)) for i in range(shards)])

    def turn(x, k):
        return lax.ppermute(x, "qry", [(i, i ^ k) for i in range(owners)])

    def collect(x):
        near = [x] + [chip(x, k) for k in range(1, half)]
        return near, [core(piece) for piece in near]

    def after(value, *others):
        return lax.optimization_barrier((value,) + others)[0]

    own_rows, _ = hidden.shape
    row_span, columns = proj_weight.shape
    passage_count, sub_count = pq_codes.shape
    queries_all = own_rows * owners
    chunk = queries_all // shards
    per_owner = own_rows // chunk

    book_rows = sub_count // shards
    book_own = codebook.reshape(shards, book_rows * 8, codebook.shape[2])
    book_slice = lax.dynamic_slice_in_dim(book_own, place, 1, 0)
    book_slices = jnp.concatenate([turn(book_slice, k) for k in range(1, owners)], axis=1)
    near, far = collect(book_slices)
    books = arrange(swapped, near + far)

    floats = hidden.astype(f32)
    inverse = lax.rsqrt(jnp.mean(floats * floats, axis=1, keepdims=True) + norm_eps)
    first = shard * row_span
    part = lax.dynamic_slice_in_dim(hidden, first, row_span, 1).astype(f32)
    part_gain = lax.dynamic_slice_in_dim(norm_gain, first, row_span, 0)
    slice_own = (part * inverse * part_gain[None, :]).astype(bf16)
    slices = [slice_own] + [turn(slice_own, k) for k in range(1, owners)]
    codes_own = pq_codes.astype(bf16).T.reshape(shards, book_rows, passage_count)
    targets = positives.reshape(shards, chunk)[swapped].reshape(1, queries_all)
    targets = (targets - shard * passage_count).astype(f32)
    source = after(owner ^ (steps // per_owner), codes_own, targets)
    goes_to = (source * per_owner + steps % per_owner) ^ place
    normed_rows = arrange(goes_to, [s.reshape(per_owner, chunk, row_span) for s in slices])
    normed_rows = normed_rows.reshape(queries_all, row_span)

    def term_of(rows):
        return jnp.dot(rows, proj_weight, preferred_element_type=f32).reshape(half, chunk, columns)

    def scatter_sum(near_term, far_term):
        arrived = core(far_term)
        summed = [near_term[k] + arrived[k] for k in range(half)]
        total = summed[0]
        for k in range(1, half):
            total = total + chip(summed[k], k)
        return total, summed

    far_part = term_of(normed_rows[half * chunk :])
    near_part = after(term_of(normed_rows[: half * chunk]))
    query_own, _ = scatter_sum(near_part, far_part)
    query_own = query_own.astype(bf16)
    first_passages = decode([codes_own], book_own, 0)

    query_blocks = jnp.stack([turn(query_own, k) for k in range(1, owners)])
    near_own, far_own = collect(query_own)
    near_queries, far_queries = collect(query_blocks)
    own_chunks = near_own + far_own

    def hop(x, pairs):
        return lax.ppermute(x, "qry", pairs)

    passages = [first_passages]
    codes = {}
    waiting = after(codes_own, query_blocks)
    for k in range(1, owners):
        if owners == 4 and k == 3:
            passed = after(codes[2][0], query_blocks)
            codes[k] = [hop(waiting, [(1, 2), (2, 1)]), hop(passed, [(1, 0), (2, 3)])]
        else:
            codes[k] = [turn(codes_own if k <= owners // 2 else waiting, k)]
        passages.append(decode(codes[k], books, k - 1))

    query_chunks = near_queries + far_queries
    scores, stats, own_rows_all = scores_of(own_chunks, query_chunks, passages, targets)
    near_stats, far_stats = collect(stats)
    score_grad, near_term, far_term, losses_all = score_grads(
        scores, near_stats + far_stats, targets, passages[0]
    )
    query_grad, grad_sums = scatter_sum(near_term, far_term)
    near_pieces, far_pieces = collect(query_grad.astype(bf16))

    passage_grad = lax.dot_general(
        own_rows_all,
        after(score_grad, grad_sums[-1]),
        (((0,), (0,)), ((), ())),
        preferred_element_type=f32,
    )
    passage_grad = (passage_grad * score_scale).astype(bf16)

    def book_of(order):
        if book_rows % 16 == 0:
            return book_grads(order, passage_grad, codes_own).reshape(
                order.shape[0], book_rows * 8, 256
            )
        group = min(sub_count, 16)
        grouped = codes_own.reshape(sub_count // group, group, passage_count)
        book = book_grads(steps[: sub_count // group], passage_grad, grouped)
        return book.reshape(shards, book_rows * 8, 256)[order]

    part = half // 2
    far_book = [core(book_of(swapped[half : half + part]))]
    both = book_of(jnp.concatenate([swapped[half + part :], swapped[part:half]]))
    far_book.append(core(both[:part]))
    near_book = [book_of(swapped[:part]), both[part:]]
    halves = [near_book[k // part][k % part] + far_book[k // part][k % part] for k in range(half)]
    book_sum = halves[0]
    for k in range(1, half):
        book_sum = book_sum + chip(halves[k].astype(bf16), k).astype(f32)
    book_sum = book_sum.astype(bf16)

    dest = ((swapped // per_owner) ^ owner) * per_owner + swapped % per_owner
    *back, grad_rows = back_part(dest, near_pieces + far_pieces, proj_weight, owners)
    weight_grad = lax.dot_general(
        normed_rows, grad_rows, (((0,), (0,)), ((), ())), preferred_element_type=f32
    )

    def rows_of(array, who):
        first = (who ^ (place // per_owner)) * own_rows
        return lax.dynamic_slice_in_dim(array, first, own_rows, 0)

    def straighten(array):
        bit = 1
        while bit < per_owner:
            shaped = array.reshape(per_owner // (2 * bit), 2, bit * chunk)
            turned = shaped[:, ::-1].reshape(array.shape)
            array = jnp.where((place // bit) % 2 == 1, turned, array)
            bit *= 2
        return array

    back_sum = back[0].astype(f32)
    for k in range(1, owners):
        back_sum = back_sum + turn(back[k], k).astype(f32)
    back_sum = back_sum.astype(bf16)
    book_shape = book_sum.shape
    shared = book_shape[0] == own_rows and row_span % book_shape[1] == 0
    books_last = None
    if shared:
        near_back, far_back = collect(jnp.concatenate([back_sum, book_sum], axis=1))
    else:
        near_back, far_back = collect(back_sum)
        books_last = sum(collect(book_sum), [])
    shard_of = (swapped % half) * 2 + swapped // half
    hidden_grad, codebook_grad = tail(
        shard_of,
        swapped,
        near_back + far_back,
        books_last,
        row_span,
        book_shape,
        hidden,
        norm_gain[None, :],
    )
    codebook_grad = codebook_grad.reshape(codebook.shape)
    losses = straighten(rows_of(losses_all[0], owner))
    return (losses, hidden_grad, weight_grad, codebook_grad)


def solution(mesh):
    rows, split = P("qry", None), P("psg", "qry")
    book = P("qry", None, None)
    return jax.shard_map(
        run_device,
        mesh=mesh,
        in_specs=(rows, P(), split, split, book, P()),
        out_specs=(P("qry"), rows, split, book),
        check_vma=False,
    )
```

```python
import functools

import jax
import jax.numpy as jnp
from jax import lax
from jax.experimental import pallas as pl
from jax.experimental.pallas import tpu as pltpu
from jax.sharding import PartitionSpec as P


score_scale = 0.0625
norm_eps = 1e-06
bf16 = jnp.bfloat16
f32 = jnp.float32


def whole(array):
    rank = len(array.shape)
    return pl.BlockSpec(array.shape, lambda *step: (0,) * rank)


def cost(flops, moved, exps=0):
    return pl.CostEstimate(flops=int(flops), bytes_accessed=int(moved), transcendentals=int(exps))


def tree(values, join=lambda a, b: a + b):
    while len(values) > 1:
        values = [join(values[i], values[i + 1]) for i in range(0, len(values), 2)]
    return values[0]


def arrange_body(count, order, *refs):
    pieces, out = refs[:-1], refs[-1]
    for c, piece in enumerate(pieces):
        for i in range(count):
            out[order[c * count + i]] = piece[i].astype(out.dtype)


def arrange(order, pieces, kind=None):
    count = pieces[0].shape[0]
    shape = (count * len(pieces),) + pieces[0].shape[1:]
    rank = len(shape)
    return pl.pallas_call(
        functools.partial(arrange_body, count),
        grid_spec=pltpu.PrefetchScalarGridSpec(
            num_scalar_prefetch=1,
            grid=(1,),
            in_specs=[whole(p) for p in pieces],
            out_specs=pl.BlockSpec(shape, lambda i, order: (0,) * rank),
        ),
        out_shape=jax.ShapeDtypeStruct(shape, kind or pieces[0].dtype),
        cost_estimate=cost(0, 8 * len(pieces) * pieces[0].size),
        name="arrange",
    )(order, *pieces)


def look_up(code, values):
    width = code.shape[1]
    full = jnp.broadcast_to(code, (8, width))
    low = full & 127
    high = full >= 128
    values = values.astype(f32)
    first, second = values[:, :128], values[:, 128:]
    pieces = []
    for c in range(width // 128):
        lanes = slice(c * 128, (c + 1) * 128)
        a = jnp.take_along_axis(first, low[:, lanes], axis=1, mode="promise_in_bounds")
        b = jnp.take_along_axis(second, low[:, lanes], axis=1, mode="promise_in_bounds")
        pieces.append(jnp.where(high[:, lanes], b, a))
    return jnp.concatenate(pieces, axis=1).astype(bf16)


def decode_body(*refs):
    parts, table, out, index = refs[:-3], refs[-3], refs[-2], refs[-1]
    slices, count, _ = index.shape
    index[...] = sum(codes[...].astype(f32) for codes in parts).astype(jnp.int32)
    for j in range(slices):
        for m in range(count):
            value = look_up(index[j, m : m + 1, :], table[j, pl.ds(m * 8, 8), :])
            out[pl.ds((j * count + m) * 8, 8), :] = value


def decode(parts, tables, layer):
    slices, count, width = parts[0].shape
    height = count * 8
    return pl.pallas_call(
        decode_body,
        grid=(slices // 2,),
        in_specs=[pl.BlockSpec((2, count, width), lambda i: (i, 0, 0)) for _ in parts]
        + [pl.BlockSpec((2, height, tables.shape[2]), lambda i: (i, layer, 0))],
        out_specs=pl.BlockSpec((2 * height, width), lambda i: (i, 0)),
        scratch_shapes=[pltpu.VMEM((2, count, width), jnp.int32)],
        out_shape=jax.ShapeDtypeStruct((slices * height, width), bf16),
        cost_estimate=cost(4 * slices * height * width * 512, slices * height * width * 2),
        name="decode",
    )(*parts, tables)


def column_of(row):
    return jnp.broadcast_to(row, (128, row.shape[1])).T


def score_body(chunks, blocks, parts, *refs):
    own, others = refs[:chunks], refs[chunks : 2 * chunks]
    rest = refs[2 * chunks :]
    tables, codes, rest = rest[: blocks - 1], rest[blocks - 1 : blocks - 1 + parts], rest[blocks - 1 + parts :]
    book, target, scores, stats, own_rows, held, places, packed, index, last_table = rest
    step, last = pl.program_id(0), pl.num_programs(0) - 1
    tile = last_table.shape[1]
    height = own[0].shape[0]
    rows = scores.shape[0]
    group = 128

    @pl.when(step == 0)
    def gather():
        for c in range(chunks):
            own_rows[pl.ds(c * height, height), :] = own[c][...]
            held[0, pl.ds(c * height, height), :] = own[c][...]
            for b in range(1, blocks):
                held[b, pl.ds(c * height, height), :] = others[c][b - 1]
        places[...] = column_of(target[...])
        packed[...] = jnp.zeros_like(packed)

    def multiply():
        index[...] = sum(code[...].astype(f32) for code in codes).astype(jnp.int32)
        slices, count = index.shape[:2]
        for j in range(slices):
            for m in range(count):
                value = look_up(index[j, m : m + 1, :], book[j, pl.ds(m * 8, 8), :])
                last_table[pl.ds((j * count + m) * 8, 8), :] = value
        total = jnp.dot(held[0], tables[0][...], preferred_element_type=f32)
        for b in range(1, blocks - 1):
            total += jnp.dot(held[b], tables[b][...], preferred_element_type=f32)
        total += jnp.dot(held[blocks - 1], last_table[...], preferred_element_type=f32)
        scores[:, pl.ds(pl.multiple_of(step * tile, tile), tile)] = total * score_scale

    def reduce(t):
        column = lax.broadcasted_iota(jnp.int32, (group, tile), 1) + t * tile
        column = column.astype(f32)
        lane = lax.broadcasted_iota(jnp.int32, (group, 128), 1) - 3 * t
        for r in range(rows // group):
            span = pl.ds(r * group, group)
            value = scores[span, pl.ds(pl.multiple_of(t * tile, tile), tile)]
            largest = jnp.max(value, axis=1, keepdims=True)
            expsum = jnp.sum(jnp.exp(value - largest), axis=1, keepdims=True)
            found = column == jnp.tile(places[span, :], (1, tile // 128))
            hit = jnp.sum(jnp.where(found, value, 0.0), axis=1, keepdims=True)
            row = jnp.where(lane == 1, expsum, jnp.where(lane == 2, hit, packed[span, :]))
            packed[span, :] = jnp.where(lane == 0, largest, row)

    @pl.when(step == 0)
    def begin():
        multiply()

    @pl.when((step > 0) & (step < last))
    def both():
        reduce(step - 1)
        multiply()

    @pl.when(step == last)
    def finish():
        reduce(last - 1)
        tiles = scores.shape[1] // tile
        for r in range(rows // group):
            span = pl.ds(r * group, group)
            turned = packed[span, :].T
            most = functools.reduce(
                jnp.maximum, [turned[3 * t : 3 * t + 1] for t in range(tiles)]
            )
            total = sum(
                turned[3 * t + 1 : 3 * t + 2] * jnp.exp(turned[3 * t : 3 * t + 1] - most)
                for t in range(tiles)
            )
            hits = sum(turned[3 * t + 2 : 3 * t + 3] for t in range(tiles))
            stats[:, span] = jnp.concatenate(
                [most, total, hits, jnp.zeros((5, group), f32)], axis=0
            )


def scores_of(own, queries, tables, codes, books, target):
    chunks, blocks = len(queries), len(tables) + 1
    height, depth = own[0].shape
    width = tables[0].shape[1]
    rows, tile = chunks * height, min(512, width)
    slices, count = codes[0].shape[:2]
    levels = books.shape[2]
    now = lambda i: jnp.minimum(i, width // tile - 1)
    return pl.pallas_call(
        functools.partial(score_body, chunks, blocks, len(codes)),
        grid=(width // tile + 1,),
        in_specs=[whole(q) for q in own + queries]
        + [pl.BlockSpec((depth, tile), lambda i: (0, now(i))) for _ in tables]
        + [pl.BlockSpec((slices, count, tile), lambda i: (0, 0, now(i))) for _ in codes]
        + [
            pl.BlockSpec((slices, count * 8, levels), lambda i: (0, blocks - 2, 0)),
            whole(target),
        ],
        out_specs=[
            pl.BlockSpec((rows, width), lambda i: (0, 0)),
            pl.BlockSpec((8, rows), lambda i: (0, 0)),
            pl.BlockSpec((rows, depth), lambda i: (0, 0)),
        ],
        out_shape=[
            jax.ShapeDtypeStruct((rows, width), f32),
            jax.ShapeDtypeStruct((8, rows), f32),
            jax.ShapeDtypeStruct((rows, depth), bf16),
        ],
        scratch_shapes=[
            pltpu.VMEM((blocks, rows, depth), bf16),
            pltpu.VMEM((rows, 128), f32),
            pltpu.VMEM((rows, 128), f32),
            pltpu.VMEM((slices, count, tile), jnp.int32),
            pltpu.VMEM((depth, tile), bf16),
        ],
        cost_estimate=cost(
            2 * rows * blocks * depth * width, blocks * depth * width * 2, rows * width
        ),
        name="scores",
    )(*own, *queries, *tables, *codes, books, target)


def shuffle(value, offset, chunk):
    count = value.shape[1] // chunk
    return jnp.concatenate(
        [value[:, (c ^ offset) * chunk : ((c ^ offset) + 1) * chunk] for c in range(count)], axis=1
    )


def grad_body(shards, *refs):
    stats = refs[:shards]
    scores, target, passages, grad, near, far, losses = refs[shards:-3]
    largest, total, places = refs[-3:]
    step, tile = pl.program_id(0), scores.shape[1]
    rows = scores.shape[0]

    @pl.when(step == 0)
    def merge():
        values = [shuffle(s[...], c, rows // shards) for c, s in enumerate(stats)]
        most = tree([v[0:1] for v in values], jnp.maximum)
        summed = tree([v[1:2] * jnp.exp(v[0:1] - most) for v in values])
        hits = tree([v[2:3] for v in values])
        losses[...] = jnp.broadcast_to(jnp.log(summed) + most - hits, losses.shape)
        largest[...] = column_of(most)
        total[...] = column_of(1.0 / summed)
        places[...] = column_of(target[...])
        near[...] = jnp.zeros_like(near)
        far[...] = jnp.zeros_like(far)

    group = 128
    for r in range(rows // group):
        span = pl.ds(r * group, group)
        shifted = scores[span, :] - jnp.tile(largest[span, :], (1, tile // 128))
        column = (lax.broadcasted_iota(jnp.int32, (group, tile), 1) + step * tile).astype(f32)
        hit = (column == jnp.tile(places[span, :], (1, tile // 128))).astype(f32)
        value = jnp.exp(shifted) * jnp.tile(total[span, :], (1, tile // 128)) - hit
        grad[span, :] = value.astype(bf16)
    term = score_scale * lax.dot_general(
        grad[...], passages[...], (((1,), (1,)), ((), ())), preferred_element_type=f32
    )
    near[...] += term[: rows // 2].reshape(near.shape)
    far[...] += term[rows // 2 :].reshape(far.shape)


def score_grads(scores, stats, target, passages):
    rows, width = scores.shape
    depth, tile = passages.shape[0], min(1024, width)
    term = (len(stats) // 2, rows // len(stats), depth)
    return pl.pallas_call(
        functools.partial(grad_body, len(stats)),
        grid=(width // tile,),
        in_specs=[whole(s) for s in stats]
        + [
            pl.BlockSpec((rows, tile), lambda i: (0, i)),
            whole(target),
            pl.BlockSpec((depth, tile), lambda i: (0, i)),
        ],
        out_specs=[
            pl.BlockSpec((rows, tile), lambda i: (0, i)),
            pl.BlockSpec(term, lambda i: (0, 0, 0)),
            pl.BlockSpec(term, lambda i: (0, 0, 0)),
            pl.BlockSpec((8, rows), lambda i: (0, 0)),
        ],
        out_shape=[
            jax.ShapeDtypeStruct((rows, width), bf16),
            jax.ShapeDtypeStruct(term, f32),
            jax.ShapeDtypeStruct(term, f32),
            jax.ShapeDtypeStruct((8, rows), f32),
        ],
        scratch_shapes=[pltpu.VMEM((rows, 128), f32)] * 3,
        cost_estimate=cost(2 * rows * width * depth, rows * width * 6, rows * width),
        name="score_grads",
    )(*stats, scores, target, passages)


def book_body(low_count, group, order, grads, codes, out, low_codes, high_codes):
    count, width = codes.shape[1], codes.shape[2]
    high_count = 256 // low_count
    code = codes[0].astype(f32)
    high = jnp.floor(code * (1.0 / low_count))
    high_codes[...] = high
    low_codes[...] = code - high * low_count
    low_iota = lax.broadcasted_iota(jnp.int32, (low_count, 128), 0).astype(f32).astype(bf16)
    high_iota = lax.broadcasted_iota(jnp.int32, (high_count * 8, 128), 0) // 8
    high_iota = high_iota.astype(f32).astype(bf16)
    low_iota = jnp.tile(low_iota, (1, width // 128))
    high_iota = jnp.tile(high_iota, (1, width // 128))
    one, zero = jnp.ones((), bf16), jnp.zeros((), bf16)
    for g in range(count // group):
        hots, masked = [], []
        for m in range(g * group, (g + 1) * group):
            low = jnp.broadcast_to(low_codes[m : m + 1, :].astype(bf16), (low_count, width))
            top = jnp.broadcast_to(high_codes[m : m + 1, :].astype(bf16), (high_count * 8, width))
            grad = jnp.tile(grads[pl.ds(m * 8, 8), :], (high_count, 1))
            hots.append(jnp.where(low == low_iota, one, zero))
            masked.append(jnp.where(top == high_iota, grad, zero))
        product = lax.dot_general(
            jnp.concatenate(masked, axis=0),
            jnp.concatenate(hots, axis=0),
            (((1,), (1,)), ((), ())),
            preferred_element_type=f32,
        )
        for i in range(group):
            height = high_count * 8
            block = product[i * height : (i + 1) * height, i * low_count : (i + 1) * low_count]
            out[g * group + i] = jnp.concatenate(
                [block[b * 8 : (b + 1) * 8, :] for b in range(high_count)], axis=1
            )


def book_grads(order, grads, codes):
    count, width = codes.shape[1:]
    slices, span = order.shape[0], count * 8
    return pl.pallas_call(
        functools.partial(book_body, 32, 4),
        grid_spec=pltpu.PrefetchScalarGridSpec(
            num_scalar_prefetch=1,
            grid=(slices,),
            in_specs=[
                pl.BlockSpec((span, width), lambda i, order: (order[i], 0)),
                pl.BlockSpec((1, count, width), lambda i, order: (order[i], 0, 0)),
            ],
            out_specs=pl.BlockSpec((count, 8, 256), lambda i, order: (i, 0, 0)),
            scratch_shapes=[pltpu.VMEM((count, width), f32), pltpu.VMEM((count, width), f32)],
        ),
        out_shape=jax.ShapeDtypeStruct((slices * count, 8, 256), f32),
        cost_estimate=cost(4 * slices * span * width * 512, slices * span * width * 2),
        name="book_grads",
    )(order, grads, codes)


def back_body(chunks, owners, order, *refs):
    pieces, weight = refs[:chunks], refs[chunks]
    outs, rows, sorted_rows = refs[chunks + 1 : -2], refs[-2], refs[-1]
    height = pieces[0].shape[0]
    for c in range(chunks):
        rows[pl.ds(c * height, height), :] = pieces[c][...]
        sorted_rows[order[c]] = pieces[c][...]
    span = rows.shape[0] // owners
    result = lax.dot_general(
        sorted_rows[...].reshape(rows.shape),
        weight[...],
        (((1,), (1,)), ((), ())),
        preferred_element_type=f32,
    ).astype(bf16)
    for k in range(owners):
        outs[k][...] = result[k * span : (k + 1) * span]


def back_part(order, pieces, weight, owners):
    height, depth = pieces[0].shape
    rows, width = height * len(pieces), weight.shape[0]
    blocks = [jax.ShapeDtypeStruct((rows // owners, width), bf16)] * owners
    return pl.pallas_call(
        functools.partial(back_body, len(pieces), owners),
        grid_spec=pltpu.PrefetchScalarGridSpec(
            num_scalar_prefetch=1,
            grid=(1,),
            in_specs=[whole(p) for p in pieces] + [whole(weight)],
            out_specs=[whole(b) for b in blocks]
            + [pl.BlockSpec((rows, depth), lambda i, order: (0, 0))],
            scratch_shapes=[pltpu.VMEM((len(pieces), height, depth), bf16)],
        ),
        out_shape=blocks + [jax.ShapeDtypeStruct((rows, depth), bf16)],
        cost_estimate=cost(2 * rows * weight.size, rows * depth * 4),
        name="back_part",
    )(order, *pieces, weight)


def tail_body(chunks, order, places, *refs):
    pieces, books = refs[:chunks], refs[chunks : 2 * chunks]
    hidden, gain, out, book_out = refs[2 * chunks :]
    for c in range(chunks):
        book_out[places[c]] = books[c][...].astype(f32)
    width = pieces[0].shape[1]
    dots, squares = [], []
    for c in range(chunks):
        lanes = pl.ds(pl.multiple_of(order[c] * width, width), width)
        value = hidden[:, lanes].astype(f32)
        scaled = pieces[c][...].astype(f32) * gain[:, lanes]
        dots.append(jnp.sum(scaled * value, axis=1, keepdims=True))
        squares.append(jnp.sum(value * value, axis=1, keepdims=True))
    count = chunks * width
    scale = lax.rsqrt(tree(squares) / count + norm_eps)
    factor = scale * scale * scale * (tree(dots) / count)
    for c in range(chunks):
        lanes = pl.ds(pl.multiple_of(order[c] * width, width), width)
        scaled = pieces[c][...].astype(f32) * gain[:, lanes]
        out[:, lanes] = (scale * scaled - hidden[:, lanes].astype(f32) * factor).astype(bf16)


def tail(order, places, pieces, books, width, book_shape, hidden, gain):
    shared = books is None
    rows = hidden.shape[0]
    book_rows, levels = book_shape
    here = width // levels if shared else 0
    book_spec = pl.BlockSpec((book_rows, levels), lambda i, order, places: (0, here))
    piece_spec = pl.BlockSpec((rows, width), lambda i, order, places: (0, 0))
    count = len(pieces)
    out_books = jax.ShapeDtypeStruct((count, book_rows, levels), f32)
    return pl.pallas_call(
        functools.partial(tail_body, count),
        grid_spec=pltpu.PrefetchScalarGridSpec(
            num_scalar_prefetch=2,
            grid=(1,),
            in_specs=[piece_spec] * count + [book_spec] * count + [whole(hidden), whole(gain)],
            out_specs=[whole(hidden), whole(out_books)],
        ),
        out_shape=[jax.ShapeDtypeStruct(hidden.shape, bf16), out_books],
        cost_estimate=cost(8 * hidden.size, hidden.size * 8),
        name="tail",
    )(order, places, *pieces, *(pieces if shared else books), hidden, gain)


def run_device(hidden, norm_gain, proj_weight, pq_codes, codebook, positives):
    shards, owners = lax.axis_size("psg"), lax.axis_size("qry")
    shard, owner = lax.axis_index("psg"), lax.axis_index("qry")
    half = shards // 2
    place = (shard % 2) * half + shard // 2
    steps = jnp.arange(shards, dtype=jnp.int32)
    swapped = steps ^ place

    def core(x):
        return lax.ppermute(x, "psg", [(i, i ^ 1) for i in range(shards)])

    def chip(x, k):
        return lax.ppermute(x, "psg", [(i, i ^ (2 * k)) for i in range(shards)])

    def turn(x, k):
        return lax.ppermute(x, "qry", [(i, i ^ k) for i in range(owners)])

    def collect(x):
        near = [x] + [chip(x, k) for k in range(1, half)]
        return near, [core(piece) for piece in near]

    def after(value, *others):
        return lax.optimization_barrier((value,) + others)[0]

    own_rows, _ = hidden.shape
    row_span, columns = proj_weight.shape
    passage_count, sub_count = pq_codes.shape
    queries_all = own_rows * owners
    chunk = queries_all // shards
    per_owner = own_rows // chunk

    book_rows = sub_count // shards
    book_own = codebook.reshape(shards, book_rows * 8, codebook.shape[2])
    book_slice = lax.dynamic_slice_in_dim(book_own, place, 1, 0)
    book_slices = jnp.concatenate([turn(book_slice, k) for k in range(1, owners)], axis=1)
    near, far = collect(book_slices)
    books = arrange(swapped, near + far)

    floats = hidden.astype(f32)
    inverse = lax.rsqrt(jnp.mean(floats * floats, axis=1, keepdims=True) + norm_eps)
    first = shard * row_span
    part = lax.dynamic_slice_in_dim(hidden, first, row_span, 1).astype(f32)
    part_gain = lax.dynamic_slice_in_dim(norm_gain, first, row_span, 0)
    slice_own = (part * inverse * part_gain[None, :]).astype(bf16)
    slices = [slice_own] + [turn(slice_own, k) for k in range(1, owners)]
    codes_own = pq_codes.astype(bf16).T.reshape(shards, book_rows, passage_count)
    targets = positives.reshape(shards, chunk)[swapped].reshape(1, queries_all)
    targets = (targets - shard * passage_count).astype(f32)
    source = after(owner ^ (steps // per_owner), codes_own, targets)
    goes_to = (source * per_owner + steps % per_owner) ^ place
    normed_rows = arrange(goes_to, [s.reshape(per_owner, chunk, row_span) for s in slices])
    normed_rows = normed_rows.reshape(queries_all, row_span)

    def term_of(rows):
        return jnp.dot(rows, proj_weight, preferred_element_type=f32).reshape(half, chunk, columns)

    def scatter_sum(near_term, far_term):
        arrived = core(far_term)
        summed = [near_term[k] + arrived[k] for k in range(half)]
        total = summed[0]
        for k in range(1, half):
            total = total + chip(summed[k], k)
        return total, summed

    far_part = term_of(normed_rows[half * chunk :])
    near_part = after(term_of(normed_rows[: half * chunk]))
    query_own, _ = scatter_sum(near_part, far_part)
    query_own = query_own.astype(bf16)
    first_passages = decode([codes_own], book_own, 0)

    query_blocks = jnp.stack([turn(query_own, k) for k in range(1, owners)])
    near_own, far_own = collect(query_own)
    near_queries, far_queries = collect(query_blocks)
    own_chunks = near_own + far_own

    def hop(x, pairs):
        return lax.ppermute(x, "qry", pairs)

    passages = [first_passages]
    codes = {}
    waiting = after(codes_own, query_blocks)
    for k in range(1, owners):
        if owners == 4 and k == 3:
            passed = after(codes[2][0], query_blocks)
            codes[k] = [hop(waiting, [(1, 2), (2, 1)]), hop(passed, [(1, 0), (2, 3)])]
        else:
            codes[k] = [turn(codes_own if k <= owners // 2 else waiting, k)]
        if k < owners - 1:
            passages.append(decode(codes[k], books, k - 1))

    query_chunks = near_queries + far_queries
    scores, stats, own_rows_all = scores_of(
        own_chunks, query_chunks, passages, codes[owners - 1], books, targets
    )
    near_stats, far_stats = collect(stats)
    score_grad, near_term, far_term, losses_all = score_grads(
        scores, near_stats + far_stats, targets, passages[0]
    )
    query_grad, grad_sums = scatter_sum(near_term, far_term)
    near_pieces, far_pieces = collect(query_grad.astype(bf16))

    passage_grad = lax.dot_general(
        own_rows_all,
        after(score_grad, grad_sums[-1]),
        (((0,), (0,)), ((), ())),
        preferred_element_type=f32,
    )
    passage_grad = (passage_grad * score_scale).astype(bf16)

    def book_of(order):
        if book_rows % 16 == 0:
            return book_grads(order, passage_grad, codes_own).reshape(
                order.shape[0], book_rows * 8, 256
            )
        group = min(sub_count, 16)
        grouped = codes_own.reshape(sub_count // group, group, passage_count)
        book = book_grads(steps[: sub_count // group], passage_grad, grouped)
        return book.reshape(shards, book_rows * 8, 256)[order]

    part = half // 2
    far_book = [core(book_of(swapped[half : half + part]))]
    both = book_of(jnp.concatenate([swapped[half + part :], swapped[part:half]]))
    far_book.append(core(both[:part]))
    near_book = [book_of(swapped[:part]), both[part:]]
    halves = [near_book[k // part][k % part] + far_book[k // part][k % part] for k in range(half)]
    book_sum = halves[0]
    for k in range(1, half):
        book_sum = book_sum + chip(halves[k].astype(bf16), k).astype(f32)
    book_sum = book_sum.astype(bf16)

    dest = ((swapped // per_owner) ^ owner) * per_owner + swapped % per_owner
    *back, grad_rows = back_part(dest, near_pieces + far_pieces, proj_weight, owners)
    weight_grad = lax.dot_general(
        normed_rows, grad_rows, (((0,), (0,)), ((), ())), preferred_element_type=f32
    )

    def rows_of(array, who):
        first = (who ^ (place // per_owner)) * own_rows
        return lax.dynamic_slice_in_dim(array, first, own_rows, 0)

    def straighten(array):
        bit = 1
        while bit < per_owner:
            shaped = array.reshape(per_owner // (2 * bit), 2, bit * chunk)
            turned = shaped[:, ::-1].reshape(array.shape)
            array = jnp.where((place // bit) % 2 == 1, turned, array)
            bit *= 2
        return array

    back_sum = back[0].astype(f32)
    for k in range(1, owners):
        back_sum = back_sum + turn(back[k], k).astype(f32)
    back_sum = back_sum.astype(bf16)
    book_shape = book_sum.shape
    shared = book_shape[0] == own_rows and row_span % book_shape[1] == 0
    books_last = None
    if shared:
        near_back, far_back = collect(jnp.concatenate([back_sum, book_sum], axis=1))
    else:
        near_back, far_back = collect(back_sum)
        books_last = sum(collect(book_sum), [])
    shard_of = (swapped % half) * 2 + swapped // half
    hidden_grad, codebook_grad = tail(
        shard_of,
        swapped,
        near_back + far_back,
        books_last,
        row_span,
        book_shape,
        hidden,
        norm_gain[None, :],
    )
    codebook_grad = codebook_grad.reshape(codebook.shape)
    losses = straighten(rows_of(losses_all[0], owner))
    return (losses, hidden_grad, weight_grad, codebook_grad)


def solution(mesh):
    rows, split = P("qry", None), P("psg", "qry")
    book = P("qry", None, None)
    return jax.shard_map(
        run_device,
        mesh=mesh,
        in_specs=(rows, P(), split, split, book, P()),
        out_specs=(P("qry"), rows, split, book),
        check_vma=False,
    )
```

```python
import functools

import jax
import jax.numpy as jnp
from jax import lax
from jax.experimental import pallas as pl
from jax.experimental.pallas import tpu as pltpu
from jax.sharding import PartitionSpec as P


score_scale = 0.0625
norm_eps = 1e-06
bf16 = jnp.bfloat16
f32 = jnp.float32


def whole(array):
    rank = len(array.shape)
    return pl.BlockSpec(array.shape, lambda *step: (0,) * rank)


def cost(flops, moved, exps=0):
    return pl.CostEstimate(flops=int(flops), bytes_accessed=int(moved), transcendentals=int(exps))


def tree(values, join=lambda a, b: a + b):
    while len(values) > 1:
        values = [join(values[i], values[i + 1]) for i in range(0, len(values), 2)]
    return values[0]


def arrange_body(count, order, *refs):
    pieces, out = refs[:-1], refs[-1]
    for c, piece in enumerate(pieces):
        for i in range(count):
            out[order[c * count + i]] = piece[i].astype(out.dtype)


def arrange(order, pieces, kind=None):
    count = pieces[0].shape[0]
    shape = (count * len(pieces),) + pieces[0].shape[1:]
    rank = len(shape)
    return pl.pallas_call(
        functools.partial(arrange_body, count),
        grid_spec=pltpu.PrefetchScalarGridSpec(
            num_scalar_prefetch=1,
            grid=(1,),
            in_specs=[whole(p) for p in pieces],
            out_specs=pl.BlockSpec(shape, lambda i, order: (0,) * rank),
        ),
        out_shape=jax.ShapeDtypeStruct(shape, kind or pieces[0].dtype),
        cost_estimate=cost(0, 8 * len(pieces) * pieces[0].size),
        name="arrange",
    )(order, *pieces)


def look_up(code, values):
    width = code.shape[1]
    full = jnp.broadcast_to(code, (8, width))
    low = full & 127
    high = full >= 128
    values = values.astype(f32)
    first, second = values[:, :128], values[:, 128:]
    pieces = []
    for c in range(width // 128):
        lanes = slice(c * 128, (c + 1) * 128)
        a = jnp.take_along_axis(first, low[:, lanes], axis=1, mode="promise_in_bounds")
        b = jnp.take_along_axis(second, low[:, lanes], axis=1, mode="promise_in_bounds")
        pieces.append(jnp.where(high[:, lanes], b, a))
    return jnp.concatenate(pieces, axis=1).astype(bf16)


def decode_body(*refs):
    parts, table, out, index = refs[:-3], refs[-3], refs[-2], refs[-1]
    slices, count, _ = index.shape
    index[...] = sum(codes[...].astype(f32) for codes in parts).astype(jnp.int32)
    for j in range(slices):
        for m in range(count):
            value = look_up(index[j, m : m + 1, :], table[j, pl.ds(m * 8, 8), :])
            out[pl.ds((j * count + m) * 8, 8), :] = value


def decode(parts, tables, layer):
    slices, count, width = parts[0].shape
    height = count * 8
    return pl.pallas_call(
        decode_body,
        grid=(slices // 2,),
        in_specs=[pl.BlockSpec((2, count, width), lambda i: (i, 0, 0)) for _ in parts]
        + [pl.BlockSpec((2, height, tables.shape[2]), lambda i: (i, layer, 0))],
        out_specs=pl.BlockSpec((2 * height, width), lambda i: (i, 0)),
        scratch_shapes=[pltpu.VMEM((2, count, width), jnp.int32)],
        out_shape=jax.ShapeDtypeStruct((slices * height, width), bf16),
        cost_estimate=cost(4 * slices * height * width * 512, slices * height * width * 2),
        name="decode",
    )(*parts, tables)


def column_of(row):
    return jnp.broadcast_to(row, (128, row.shape[1])).T


def score_body(chunks, blocks, parts, *refs):
    own, others = refs[:chunks], refs[chunks : 2 * chunks]
    rest = refs[2 * chunks :]
    tables, codes, rest = rest[: blocks - 1], rest[blocks - 1 : blocks - 1 + parts], rest[blocks - 1 + parts :]
    book, target, scores, stats, own_rows, held, places, packed, index, last_table = rest
    step, last = pl.program_id(0), pl.num_programs(0) - 1
    tile = last_table.shape[1]
    height = own[0].shape[0]
    rows = scores.shape[0]
    group = 128

    @pl.when(step == 0)
    def gather():
        for c in range(chunks):
            own_rows[pl.ds(c * height, height), :] = own[c][...]
            held[0, pl.ds(c * height, height), :] = own[c][...]
            for b in range(1, blocks):
                held[b, pl.ds(c * height, height), :] = others[c][b - 1]
        places[...] = column_of(target[...])
        packed[...] = jnp.zeros_like(packed)

    def multiply():
        index[...] = sum(code[...].astype(f32) for code in codes).astype(jnp.int32)
        slices, count = index.shape[:2]
        for j in range(slices):
            for m in range(count):
                value = look_up(index[j, m : m + 1, :], book[j, pl.ds(m * 8, 8), :])
                last_table[pl.ds((j * count + m) * 8, 8), :] = value
        total = jnp.dot(held[0], tables[0][...], preferred_element_type=f32)
        for b in range(1, blocks - 1):
            total += jnp.dot(held[b], tables[b][...], preferred_element_type=f32)
        total += jnp.dot(held[blocks - 1], last_table[...], preferred_element_type=f32)
        scores[:, pl.ds(pl.multiple_of(step * tile, tile), tile)] = total * score_scale

    def reduce(t):
        column = lax.broadcasted_iota(jnp.int32, (group, tile), 1) + t * tile
        column = column.astype(f32)
        lane = lax.broadcasted_iota(jnp.int32, (group, 128), 1) - 3 * t
        for r in range(rows // group):
            span = pl.ds(r * group, group)
            value = scores[span, pl.ds(pl.multiple_of(t * tile, tile), tile)]
            largest = jnp.max(value, axis=1, keepdims=True)
            expsum = jnp.sum(jnp.exp(value - largest), axis=1, keepdims=True)
            found = column == jnp.tile(places[span, :], (1, tile // 128))
            hit = jnp.sum(jnp.where(found, value, 0.0), axis=1, keepdims=True)
            row = jnp.where(lane == 1, expsum, jnp.where(lane == 2, hit, packed[span, :]))
            packed[span, :] = jnp.where(lane == 0, largest, row)

    @pl.when(step == 0)
    def begin():
        multiply()

    @pl.when((step > 0) & (step < last))
    def both():
        reduce(step - 1)
        multiply()

    @pl.when(step == last)
    def finish():
        reduce(last - 1)
        tiles = scores.shape[1] // tile
        for r in range(rows // group):
            span = pl.ds(r * group, group)
            turned = packed[span, :].T
            most = functools.reduce(
                jnp.maximum, [turned[3 * t : 3 * t + 1] for t in range(tiles)]
            )
            total = sum(
                turned[3 * t + 1 : 3 * t + 2] * jnp.exp(turned[3 * t : 3 * t + 1] - most)
                for t in range(tiles)
            )
            hits = sum(turned[3 * t + 2 : 3 * t + 3] for t in range(tiles))
            stats[:, span] = jnp.concatenate(
                [most, total, hits, jnp.zeros((5, group), f32)], axis=0
            )


def scores_of(own, queries, tables, codes, books, target):
    chunks, blocks = len(queries), len(tables) + 1
    height, depth = own[0].shape
    width = tables[0].shape[1]
    rows, tile = chunks * height, min(512, width)
    slices, count = codes[0].shape[:2]
    levels = books.shape[2]
    now = lambda i: jnp.minimum(i, width // tile - 1)
    return pl.pallas_call(
        functools.partial(score_body, chunks, blocks, len(codes)),
        grid=(width // tile + 1,),
        in_specs=[whole(q) for q in own + queries]
        + [pl.BlockSpec((depth, tile), lambda i: (0, now(i))) for _ in tables]
        + [pl.BlockSpec((slices, count, tile), lambda i: (0, 0, now(i))) for _ in codes]
        + [
            pl.BlockSpec((slices, count * 8, levels), lambda i: (0, blocks - 2, 0)),
            whole(target),
        ],
        out_specs=[
            pl.BlockSpec((rows, width), lambda i: (0, 0)),
            pl.BlockSpec((8, rows), lambda i: (0, 0)),
            pl.BlockSpec((rows, depth), lambda i: (0, 0)),
        ],
        out_shape=[
            jax.ShapeDtypeStruct((rows, width), f32),
            jax.ShapeDtypeStruct((8, rows), f32),
            jax.ShapeDtypeStruct((rows, depth), bf16),
        ],
        scratch_shapes=[
            pltpu.VMEM((blocks, rows, depth), bf16),
            pltpu.VMEM((rows, 128), f32),
            pltpu.VMEM((rows, 128), f32),
            pltpu.VMEM((slices, count, tile), jnp.int32),
            pltpu.VMEM((depth, tile), bf16),
        ],
        cost_estimate=cost(
            2 * rows * blocks * depth * width, blocks * depth * width * 2, rows * width
        ),
        name="scores",
    )(*own, *queries, *tables, *codes, books, target)


def shuffle(value, offset, chunk):
    count = value.shape[1] // chunk
    return jnp.concatenate(
        [value[:, (c ^ offset) * chunk : ((c ^ offset) + 1) * chunk] for c in range(count)], axis=1
    )


def grad_body(shards, *refs):
    stats = refs[:shards]
    scores, target, passages, grad, near, far, losses = refs[shards:-3]
    largest, total, places = refs[-3:]
    step, tile = pl.program_id(0), scores.shape[1]
    rows = scores.shape[0]

    @pl.when(step == 0)
    def merge():
        values = [shuffle(s[...], c, rows // shards) for c, s in enumerate(stats)]
        most = tree([v[0:1] for v in values], jnp.maximum)
        summed = tree([v[1:2] * jnp.exp(v[0:1] - most) for v in values])
        hits = tree([v[2:3] for v in values])
        losses[...] = jnp.broadcast_to(jnp.log(summed) + most - hits, losses.shape)
        largest[...] = column_of(most)
        total[...] = column_of(1.0 / summed)
        places[...] = column_of(target[...])
        near[...] = jnp.zeros_like(near)
        far[...] = jnp.zeros_like(far)

    group = 128
    for r in range(rows // group):
        span = pl.ds(r * group, group)
        shifted = scores[span, :] - jnp.tile(largest[span, :], (1, tile // 128))
        column = (lax.broadcasted_iota(jnp.int32, (group, tile), 1) + step * tile).astype(f32)
        hit = (column == jnp.tile(places[span, :], (1, tile // 128))).astype(f32)
        value = jnp.exp(shifted) * jnp.tile(total[span, :], (1, tile // 128)) - hit
        grad[span, :] = value.astype(bf16)
    term = score_scale * lax.dot_general(
        grad[...], passages[...], (((1,), (1,)), ((), ())), preferred_element_type=f32
    )
    near[...] += term[: rows // 2].reshape(near.shape)
    far[...] += term[rows // 2 :].reshape(far.shape)


def score_grads(scores, stats, target, passages):
    rows, width = scores.shape
    depth, tile = passages.shape[0], min(1024, width)
    term = (len(stats) // 2, rows // len(stats), depth)
    return pl.pallas_call(
        functools.partial(grad_body, len(stats)),
        grid=(width // tile,),
        in_specs=[whole(s) for s in stats]
        + [
            pl.BlockSpec((rows, tile), lambda i: (0, i)),
            whole(target),
            pl.BlockSpec((depth, tile), lambda i: (0, i)),
        ],
        out_specs=[
            pl.BlockSpec((rows, tile), lambda i: (0, i)),
            pl.BlockSpec(term, lambda i: (0, 0, 0)),
            pl.BlockSpec(term, lambda i: (0, 0, 0)),
            pl.BlockSpec((8, rows), lambda i: (0, 0)),
        ],
        out_shape=[
            jax.ShapeDtypeStruct((rows, width), bf16),
            jax.ShapeDtypeStruct(term, f32),
            jax.ShapeDtypeStruct(term, f32),
            jax.ShapeDtypeStruct((8, rows), f32),
        ],
        scratch_shapes=[pltpu.VMEM((rows, 128), f32)] * 3,
        cost_estimate=cost(2 * rows * width * depth, rows * width * 6, rows * width),
        name="score_grads",
    )(*stats, scores, target, passages)


def book_body(low_count, group, order, grads, codes, out, low_codes, high_codes):
    count, width = codes.shape[1], codes.shape[2]
    high_count = 256 // low_count
    code = codes[0].astype(f32)
    high = jnp.floor(code * (1.0 / low_count))
    high_codes[...] = high
    low_codes[...] = code - high * low_count
    low_iota = lax.broadcasted_iota(jnp.int32, (low_count, 128), 0).astype(f32).astype(bf16)
    high_iota = lax.broadcasted_iota(jnp.int32, (high_count * 8, 128), 0) // 8
    high_iota = high_iota.astype(f32).astype(bf16)
    low_iota = jnp.tile(low_iota, (1, width // 128))
    high_iota = jnp.tile(high_iota, (1, width // 128))
    one, zero = jnp.ones((), bf16), jnp.zeros((), bf16)
    for g in range(count // group):
        hots, masked = [], []
        for m in range(g * group, (g + 1) * group):
            low = jnp.broadcast_to(low_codes[m : m + 1, :].astype(bf16), (low_count, width))
            top = jnp.broadcast_to(high_codes[m : m + 1, :].astype(bf16), (high_count * 8, width))
            grad = jnp.tile(grads[pl.ds(m * 8, 8), :], (high_count, 1))
            hots.append(jnp.where(low == low_iota, one, zero))
            masked.append(jnp.where(top == high_iota, grad, zero))
        product = lax.dot_general(
            jnp.concatenate(masked, axis=0),
            jnp.concatenate(hots, axis=0),
            (((1,), (1,)), ((), ())),
            preferred_element_type=f32,
        )
        for i in range(group):
            height = high_count * 8
            block = product[i * height : (i + 1) * height, i * low_count : (i + 1) * low_count]
            out[g * group + i] = jnp.concatenate(
                [block[b * 8 : (b + 1) * 8, :] for b in range(high_count)], axis=1
            )


def book_grads(order, grads, codes):
    count, width = codes.shape[1:]
    slices, span = order.shape[0], count * 8
    return pl.pallas_call(
        functools.partial(book_body, 32, 4),
        grid_spec=pltpu.PrefetchScalarGridSpec(
            num_scalar_prefetch=1,
            grid=(slices,),
            in_specs=[
                pl.BlockSpec((span, width), lambda i, order: (order[i], 0)),
                pl.BlockSpec((1, count, width), lambda i, order: (order[i], 0, 0)),
            ],
            out_specs=pl.BlockSpec((count, 8, 256), lambda i, order: (i, 0, 0)),
            scratch_shapes=[pltpu.VMEM((count, width), f32), pltpu.VMEM((count, width), f32)],
        ),
        out_shape=jax.ShapeDtypeStruct((slices * count, 8, 256), f32),
        cost_estimate=cost(4 * slices * span * width * 512, slices * span * width * 2),
        name="book_grads",
    )(order, grads, codes)


def back_body(chunks, owners, order, *refs):
    pieces, weight = refs[:chunks], refs[chunks]
    outs, rows, sorted_rows = refs[chunks + 1 : -2], refs[-2], refs[-1]
    height = pieces[0].shape[0]
    for c in range(chunks):
        rows[pl.ds(c * height, height), :] = pieces[c][...]
        sorted_rows[order[c]] = pieces[c][...]
    span = rows.shape[0] // owners
    result = lax.dot_general(
        sorted_rows[...].reshape(rows.shape),
        weight[...],
        (((1,), (1,)), ((), ())),
        preferred_element_type=f32,
    ).astype(bf16)
    for k in range(owners):
        outs[k][...] = result[k * span : (k + 1) * span]


def back_part(order, pieces, weight, owners):
    height, depth = pieces[0].shape
    rows, width = height * len(pieces), weight.shape[0]
    blocks = [jax.ShapeDtypeStruct((rows // owners, width), bf16)] * owners
    return pl.pallas_call(
        functools.partial(back_body, len(pieces), owners),
        grid_spec=pltpu.PrefetchScalarGridSpec(
            num_scalar_prefetch=1,
            grid=(1,),
            in_specs=[whole(p) for p in pieces] + [whole(weight)],
            out_specs=[whole(b) for b in blocks]
            + [pl.BlockSpec((rows, depth), lambda i, order: (0, 0))],
            scratch_shapes=[pltpu.VMEM((len(pieces), height, depth), bf16)],
        ),
        out_shape=blocks + [jax.ShapeDtypeStruct((rows, depth), bf16)],
        cost_estimate=cost(2 * rows * weight.size, rows * depth * 4),
        name="back_part",
    )(order, *pieces, weight)


def tail_body(chunks, order, places, *refs):
    pieces, books = refs[:chunks], refs[chunks : 2 * chunks]
    hidden, gain, out, book_out = refs[2 * chunks :]
    for c in range(chunks):
        book_out[places[c]] = books[c][...].astype(f32)
    width = pieces[0].shape[1]
    dots, squares = [], []
    for c in range(chunks):
        lanes = pl.ds(pl.multiple_of(order[c] * width, width), width)
        value = hidden[:, lanes].astype(f32)
        scaled = pieces[c][...].astype(f32) * gain[:, lanes]
        dots.append(jnp.sum(scaled * value, axis=1, keepdims=True))
        squares.append(jnp.sum(value * value, axis=1, keepdims=True))
    count = chunks * width
    scale = lax.rsqrt(tree(squares) / count + norm_eps)
    factor = scale * scale * scale * (tree(dots) / count)
    for c in range(chunks):
        lanes = pl.ds(pl.multiple_of(order[c] * width, width), width)
        scaled = pieces[c][...].astype(f32) * gain[:, lanes]
        out[:, lanes] = (scale * scaled - hidden[:, lanes].astype(f32) * factor).astype(bf16)


def tail(order, places, pieces, books, width, book_shape, hidden, gain):
    shared = books is None
    rows = hidden.shape[0]
    book_rows, levels = book_shape
    here = width // levels if shared else 0
    book_spec = pl.BlockSpec((book_rows, levels), lambda i, order, places: (0, here))
    piece_spec = pl.BlockSpec((rows, width), lambda i, order, places: (0, 0))
    count = len(pieces)
    out_books = jax.ShapeDtypeStruct((count, book_rows, levels), f32)
    return pl.pallas_call(
        functools.partial(tail_body, count),
        grid_spec=pltpu.PrefetchScalarGridSpec(
            num_scalar_prefetch=2,
            grid=(1,),
            in_specs=[piece_spec] * count + [book_spec] * count + [whole(hidden), whole(gain)],
            out_specs=[whole(hidden), whole(out_books)],
        ),
        out_shape=[jax.ShapeDtypeStruct(hidden.shape, bf16), out_books],
        cost_estimate=cost(8 * hidden.size, hidden.size * 8),
        name="tail",
    )(order, places, *pieces, *(pieces if shared else books), hidden, gain)


def run_device(hidden, norm_gain, proj_weight, pq_codes, codebook, positives):
    shards, owners = lax.axis_size("psg"), lax.axis_size("qry")
    shard, owner = lax.axis_index("psg"), lax.axis_index("qry")
    half = shards // 2
    place = (shard % 2) * half + shard // 2
    steps = jnp.arange(shards, dtype=jnp.int32)
    swapped = steps ^ place

    def core(x):
        return lax.ppermute(x, "psg", [(i, i ^ 1) for i in range(shards)])

    def chip(x, k):
        return lax.ppermute(x, "psg", [(i, i ^ (2 * k)) for i in range(shards)])

    def turn(x, k):
        return lax.ppermute(x, "qry", [(i, i ^ k) for i in range(owners)])

    def collect(x):
        near = [x] + [chip(x, k) for k in range(1, half)]
        return near, [core(piece) for piece in near]

    def after(value, *others):
        return lax.optimization_barrier((value,) + others)[0]

    own_rows, _ = hidden.shape
    row_span, columns = proj_weight.shape
    passage_count, sub_count = pq_codes.shape
    queries_all = own_rows * owners
    chunk = queries_all // shards
    per_owner = own_rows // chunk

    book_rows = sub_count // shards
    book_own = codebook.reshape(shards, book_rows * 8, codebook.shape[2])
    book_slice = lax.dynamic_slice_in_dim(book_own, place, 1, 0)
    book_slices = jnp.concatenate([turn(book_slice, k) for k in range(1, owners)], axis=1)
    near, far = collect(book_slices)
    books = arrange(swapped, near + far)

    floats = hidden.astype(f32)
    inverse = lax.rsqrt(jnp.mean(floats * floats, axis=1, keepdims=True) + norm_eps)
    first = shard * row_span
    part = lax.dynamic_slice_in_dim(hidden, first, row_span, 1).astype(f32)
    part_gain = lax.dynamic_slice_in_dim(norm_gain, first, row_span, 0)
    slice_own = (part * inverse * part_gain[None, :]).astype(bf16)
    slices = [slice_own] + [turn(slice_own, k) for k in range(1, owners)]
    codes_own = pq_codes.astype(bf16).T.reshape(shards, book_rows, passage_count)
    targets = positives.reshape(shards, chunk)[swapped].reshape(1, queries_all)
    targets = (targets - shard * passage_count).astype(f32)
    source = after(owner ^ (steps // per_owner), codes_own, targets)
    goes_to = (source * per_owner + steps % per_owner) ^ place
    normed_rows = arrange(goes_to, [s.reshape(per_owner, chunk, row_span) for s in slices])
    normed_rows = normed_rows.reshape(queries_all, row_span)

    def term_of(rows):
        return jnp.dot(rows, proj_weight, preferred_element_type=f32).reshape(half, chunk, columns)

    def scatter_sum(near_term, far_term):
        arrived = core(far_term)
        summed = [near_term[k] + arrived[k] for k in range(half)]
        total = summed[0]
        for k in range(1, half):
            total = total + chip(summed[k], k)
        return total, summed

    far_part = term_of(normed_rows[half * chunk :])
    near_part = after(term_of(normed_rows[: half * chunk]))
    query_own, _ = scatter_sum(near_part, far_part)
    query_own = query_own.astype(bf16)
    first_passages = decode([codes_own], book_own, 0)

    query_blocks = jnp.stack([turn(query_own, k) for k in range(1, owners)])
    near_own, far_own = collect(query_own)
    near_queries, far_queries = collect(query_blocks)
    own_chunks = near_own + far_own

    def hop(x, pairs):
        return lax.ppermute(x, "qry", pairs)

    passages = [first_passages]
    codes = {}
    waiting = after(codes_own, query_blocks)
    for k in range(1, owners):
        if owners == 4 and k == 3:
            passed = after(codes[2][0], query_blocks)
            codes[k] = [hop(waiting, [(1, 2), (2, 1)]), hop(passed, [(1, 0), (2, 3)])]
        else:
            codes[k] = [turn(codes_own if k <= owners // 2 else waiting, k)]
        if k < owners - 1:
            passages.append(decode(codes[k], books, k - 1))

    query_chunks = near_queries + far_queries
    scores, stats, own_rows_all = scores_of(
        own_chunks, query_chunks, passages, codes[owners - 1], books, targets
    )
    near_stats, far_stats = collect(stats)
    score_grad, near_term, far_term, losses_all = score_grads(
        scores, near_stats + far_stats, targets, passages[0]
    )
    query_grad, grad_sums = scatter_sum(near_term, far_term)
    near_pieces, far_pieces = collect(query_grad.astype(bf16))

    passage_grad = lax.dot_general(
        own_rows_all,
        after(score_grad, grad_sums[-1]),
        (((0,), (0,)), ((), ())),
        preferred_element_type=f32,
    )
    passage_grad = (passage_grad * score_scale).astype(bf16)

    def book_of(order):
        if book_rows % 16 == 0:
            return book_grads(order, passage_grad, codes_own).reshape(
                order.shape[0], book_rows * 8, 256
            )
        group = min(sub_count, 16)
        grouped = codes_own.reshape(sub_count // group, group, passage_count)
        book = book_grads(steps[: sub_count // group], passage_grad, grouped)
        return book.reshape(shards, book_rows * 8, 256)[order]

    part = half // 2
    far_book = [core(book_of(swapped[half : half + part]))]
    both = book_of(jnp.concatenate([swapped[half + part :], swapped[1:half]]))
    far_book.append(core(both[: half - part]))
    near_book = [book_of(swapped[:1])[0]] + [both[half - part + k] for k in range(half - 1)]
    halves = [near_book[k] + far_book[k // part][k % part] for k in range(half)]
    book_sum = halves[0]
    for k in range(1, half):
        book_sum = book_sum + chip(halves[k].astype(bf16), k).astype(f32)
    book_sum = book_sum.astype(bf16)

    dest = ((swapped // per_owner) ^ owner) * per_owner + swapped % per_owner
    *back, grad_rows = back_part(dest, near_pieces + far_pieces, proj_weight, owners)
    weight_grad = lax.dot_general(
        normed_rows, grad_rows, (((0,), (0,)), ((), ())), preferred_element_type=f32
    )

    def rows_of(array, who):
        first = (who ^ (place // per_owner)) * own_rows
        return lax.dynamic_slice_in_dim(array, first, own_rows, 0)

    def straighten(array):
        bit = 1
        while bit < per_owner:
            shaped = array.reshape(per_owner // (2 * bit), 2, bit * chunk)
            turned = shaped[:, ::-1].reshape(array.shape)
            array = jnp.where((place // bit) % 2 == 1, turned, array)
            bit *= 2
        return array

    back_sum = back[0].astype(f32)
    for k in range(1, owners):
        back_sum = back_sum + turn(back[k], k).astype(f32)
    back_sum = back_sum.astype(bf16)
    book_shape = book_sum.shape
    shared = book_shape[0] == own_rows and row_span % book_shape[1] == 0
    books_last = None
    if shared:
        near_back, far_back = collect(jnp.concatenate([back_sum, book_sum], axis=1))
    else:
        near_back, far_back = collect(back_sum)
        books_last = sum(collect(book_sum), [])
    shard_of = (swapped % half) * 2 + swapped // half
    hidden_grad, codebook_grad = tail(
        shard_of,
        swapped,
        near_back + far_back,
        books_last,
        row_span,
        book_shape,
        hidden,
        norm_gain[None, :],
    )
    codebook_grad = codebook_grad.reshape(codebook.shape)
    losses = straighten(rows_of(losses_all[0], owner))
    return (losses, hidden_grad, weight_grad, codebook_grad)


def solution(mesh):
    rows, split = P("qry", None), P("psg", "qry")
    book = P("qry", None, None)
    return jax.shard_map(
        run_device,
        mesh=mesh,
        in_specs=(rows, P(), split, split, book, P()),
        out_specs=(P("qry"), rows, split, book),
        check_vma=False,
    )
```
